768 devices in a mesh: ctx: 48 (over x, z_lo, core), tp: 16 (over y, z_hi).
Axes of the slice: x: 4, y: 8, z: 12 (z_hi: 2, z_lo: 6; z = z_hi * 6 + z_lo), core: 2. Of those that a mesh axis runs over, the one named last changes fastest.
Arguments:
- queries: bfloat16 [18432, 2048], P('ctx', 'tp'), may hold values from -8 to 8
- key_rows: bfloat16 [18432, 2048], P('ctx', 'tp'), may hold values from -8 to 8
- values: bfloat16 [18432, 2048], P('ctx', 'tp'), may hold values from -6 to 6
- cotangent: bfloat16 [18432, 4096], P('ctx', 'tp'), may hold values from -1.5 to 1.5
- w_flat: bfloat16 [16, 4128, 128], P('tp', 'ctx'), may hold values from -0.125 to 0.125
- block_keys: int32 [144, 6], P('ctx'), may hold values from 0 to 143, as said below
Outputs:
- query_grad: float32 [18432, 2048], P('ctx', 'tp')
- key_grad: float32 [18432, 2048], P('ctx', 'tp')
- value_grad: float32 [18432, 2048], P('ctx', 'tp')
- weight_grad: float32 [16, 4128, 128], P('tp', 'ctx')
The draws below stay inside these ranges and needn't reach their ends.
Inputs may be any that keep to these rules, and one draw needn't show every extreme that they name: `block_keys`: row b lists b, then b - 1 and b + 1 modulo 144, then for k = 1, 2, 3 a block c whose c - c % 3 equals (b - b % 3 + k * 36) modulo 144.
All inputs are finite; a program needn't handle non-finite values.
Results may differ from the reference program's by a relative error of at most 0.034.
Values may be sent and summed in bfloat16 or wider, within the bound.
No kernel may reach another device: no remote copies, remote signals or barrier semaphores. Data moves between devices by JAX's collectives and lax.ppermute only.
A program may use at most 32 MiB of HBM per device.

```python
import jax
import jax.numpy as jnp
from jax import lax

D = 4096
DH = 128
HEADS = 16
BLK = 128
NSEL = 6
BLK_DEV = 3
TOKENS = 18432
NB = 144
SPAN = 36
HW = 2048
FLAT_ROWS = 4096
SHARD = 86
N_CTX = 48
N_TP = 16


def draw_queries(key, part):
    drawn = 1.5 * jax.random.normal(jax.random.fold_in(key, 1), (TOKENS, HW), jnp.float32)
    return jnp.clip(drawn, -8.0, 8.0).astype(jnp.bfloat16)


def draw_key_rows(key, part):
    drawn = jax.random.normal(jax.random.fold_in(key, 2), (TOKENS, HW), jnp.float32)
    return jnp.clip(drawn, -8.0, 8.0).astype(jnp.bfloat16)


def draw_block_keys(key, part):
    rows = jnp.arange(NB, dtype=jnp.int32)
    starts = rows - rows % BLK_DEV
    picked = jax.random.randint(key, (NB, 3), 0, BLK_DEV, dtype=jnp.int32)
    strides = jnp.arange(1, 4, dtype=jnp.int32) * SPAN
    distant = (starts[:, None] + strides[None, :]) % NB + picked
    band_keys = jnp.stack([rows, (rows - 1) % NB, (rows + 1) % NB], axis=1)
    return jnp.concatenate([band_keys, distant], axis=1).astype(jnp.int32)


def steps_of(rng, shape, cuts, low, high):
    level = 1.0
    for position, parts in cuts:
        heights = jax.random.uniform(jax.random.fold_in(jax.random.fold_in(rng, 6), position), (parts,), jnp.float32, low / len(cuts), high / len(cuts))
        level = level * jnp.repeat(jnp.exp(heights), shape[position] // parts).reshape((-1,) + (1,) * (len(shape) - 1 - position))
    return level


def gaussian(stream_key, extent, deviation, limit, cuts=(), kind=jnp.bfloat16):
    entries = jax.random.normal(stream_key, extent, jnp.float32) * deviation
    if len(cuts) > 0:
        entries = steps_of(stream_key, extent, cuts, -0.22, 0.18) * entries
    return jnp.clip(entries, min=-limit, max=limit).astype(kind)


def setup_inputs(seed: int = 0) -> dict:
    splits = jax.random.split(jax.random.key(seed), 7)
    queries = draw_queries(jax.random.fold_in(splits[6], 71), 0)
    key_rows = draw_key_rows(jax.random.fold_in(splits[6], 71), 0)
    values = gaussian(splits[2], (TOKENS, HW), 1.0, 6.0, ((0, 48), (1, 16)))
    cotangent = gaussian(splits[3], (TOKENS, D), 0.25, 1.5, ((0, 48), (1, 16)))
    w_flat = gaussian(splits[4], (N_TP, N_CTX * SHARD, 128), HW ** -0.5, 0.125, ((0, 16), (1, 48)))
    block_keys = draw_block_keys(jax.random.fold_in(splits[6], 71), 0)
    return {"queries": queries, "key_rows": key_rows, "values": values, "cotangent": cotangent, "w_flat": w_flat, "block_keys": block_keys}


def reference(queries, key_rows, values, cotangent, w_flat, block_keys):
    score_scale = DH ** -0.5
    weight = w_flat[:, :FLAT_ROWS, :].reshape(HW, D)
    q_blocks = queries.reshape(NB, BLK, HEADS, DH)
    k_blocks = key_rows.reshape(NB, BLK, HEADS, DH)
    v_blocks = values.reshape(NB, BLK, HEADS, DH)

    def softmax_block(block_index):
        chosen = block_keys[block_index]
        key_sel = k_blocks[chosen].reshape(NSEL * BLK, HEADS, DH).astype(jnp.float32)
        val_sel = v_blocks[chosen].reshape(NSEL * BLK, HEADS, DH).astype(jnp.float32)
        query_now = q_blocks[block_index].astype(jnp.float32)
        scores = jnp.einsum("qhd,khd->hqk", query_now, key_sel) * score_scale
        row_max = jnp.max(scores, axis=-1, keepdims=True)
        exp_terms = jnp.exp(scores - row_max)
        probs = exp_terms / jnp.sum(exp_terms, axis=-1, keepdims=True)
        probs_low = lax.optimization_barrier(probs.astype(jnp.bfloat16)).astype(jnp.float32)
        return chosen, query_now, key_sel, val_sel, probs, probs_low

    def forward_block(block_index):
        chosen, query_now, key_sel, val_sel, probs, probs_low = softmax_block(block_index)
        return jnp.einsum("hqk,khd->qhd", probs_low, val_sel).astype(jnp.bfloat16)

    attended = lax.map(forward_block, jnp.arange(NB, dtype=jnp.int32))
    attn_rows = attended.reshape(TOKENS, HW)
    out_grad = jnp.dot(cotangent, weight.T, preferred_element_type=jnp.float32).astype(jnp.bfloat16)
    weight_term = jnp.dot(attn_rows.T, cotangent, preferred_element_type=jnp.float32)
    flat_grad = weight_term.reshape(N_TP, FLAT_ROWS, 128)
    weight_grad = jnp.zeros((N_TP, N_CTX * SHARD, 128), jnp.float32).at[:, :FLAT_ROWS].set(flat_grad)
    grad_blocks = out_grad.reshape(NB, BLK, HEADS, DH)

    def backward_block(totals, block_index):
        key_acc, val_acc = totals
        chosen, query_now, key_sel, val_sel, probs, probs_low = softmax_block(block_index)
        attn_now = attended[block_index].astype(jnp.float32)
        grad_now = grad_blocks[block_index].astype(jnp.float32)
        delta_rows = jnp.transpose(jnp.sum(grad_now * attn_now, axis=-1))[:, :, None]
        prob_grad = jnp.einsum("qhd,khd->hqk", grad_now, val_sel)
        score_grad = lax.optimization_barrier((probs * (prob_grad - delta_rows)).astype(jnp.bfloat16)).astype(jnp.float32)
        query_part = jnp.einsum("hqk,khd->qhd", score_grad, key_sel) * score_scale
        key_part = jnp.einsum("hqk,qhd->khd", score_grad, query_now) * score_scale
        value_part = jnp.einsum("hqk,qhd->khd", probs_low, grad_now)
        key_acc = key_acc.at[chosen].add(key_part.reshape(NSEL, BLK, HEADS, DH))
        val_acc = val_acc.at[chosen].add(value_part.reshape(NSEL, BLK, HEADS, DH))
        return (key_acc, val_acc), query_part

    empty_acc = jnp.zeros((NB, BLK, HEADS, DH), jnp.float32)
    (key_acc, val_acc), query_parts = lax.scan(backward_block, (empty_acc, empty_acc), jnp.arange(NB, dtype=jnp.int32))
    return (query_parts.reshape(TOKENS, HW), key_acc.reshape(TOKENS, HW), val_acc.reshape(TOKENS, HW), weight_grad)
```

```python
import jax
import jax.numpy as jnp
from jax import lax
from jax.experimental import pallas as pl
from jax.experimental.pallas import tpu as pltpu
from jax.sharding import PartitionSpec as P

DH = 128
BLK = 128
F32 = jnp.float32
BF16 = jnp.bfloat16

NX, NZ, NY = 4, 6, 8
N_CTX = NX * NZ * 2
N_TP = NY * 2
CHIPS = NX * NZ
SHARD = 86
SHARD_PAD = 88
FLAT_ROWS = 4096
WCOL = 256
SAME_CORE = [[2 * i + core for i in range(CHIPS)] for core in range(2)]
X_GROUPS = [[x * NZ * 2 + rest for x in range(NX)] for rest in range(NZ * 2)]
Y_GROUPS = [[2 * y + z for y in range(NY)] for z in range(2)]
SMEM = pl.BlockSpec(memory_space=pltpu.SMEM)
VMEM = pl.BlockSpec(memory_space=pltpu.VMEM)
PARAMS = pltpu.CompilerParams(vmem_limit_bytes=48 * 1024 * 1024)

M_X, M_CORE, M_Y, M_Z = 9, 10, 11, 12


def dot(a, b, ca, cb):
    return lax.dot_general(a, b, (((ca,), (cb,)), ((), ())), preferred_element_type=F32)


def ctx_shift(value, steps):
    return lax.ppermute(value, "ctx", [(s, (s + steps) % N_CTX) for s in range(N_CTX)])


def core_swap(value):
    return lax.ppermute(value, "ctx", [(s, s ^ 1) for s in range(N_CTX)])


def twin_swap(value):
    return lax.ppermute(value, "tp", [(s, s ^ 1) for s in range(N_TP)])


def y_shift(value, steps):
    pairs = [(2 * y + z, 2 * ((y + steps) % NY) + z) for y in range(NY) for z in range(2)]
    return lax.ppermute(value, "tp", pairs)


def select(meta, j, which, kv, prev, nxt, far):
    parts = [kv[which, j * BLK : (j + 1) * BLK]]
    parts.append(prev[which] if j == 0 else kv[which, (j - 1) * BLK : j * BLK])
    parts.append(nxt[which] if j == 2 else kv[which, (j + 1) * BLK : (j + 2) * BLK])
    for k in range(3):
        source = (meta[M_X] + k + 1) % NX
        row = pl.multiple_of(meta[3 * j + k] * BLK, BLK)
        parts.append(far[source, which, pl.ds(row, BLK)])
    return jnp.concatenate(parts, axis=0)


def forward_kernel(meta, q, kv, prev, nxt, far, probs_out, att_out):
    for j in range(3):
        rows = slice(j * BLK, (j + 1) * BLK)
        keys = select(meta, j, 0, kv, prev, nxt, far)
        vals = select(meta, j, 1, kv, prev, nxt, far)
        scores = dot(q[rows], keys, 1, 1) * (DH**-0.5)
        terms = jnp.exp(scores - jnp.max(scores, axis=-1, keepdims=True))
        probs = terms / jnp.sum(terms, axis=-1, keepdims=True)
        probs_out[j] = probs
        att_out[rows] = dot(probs.astype(BF16), vals, 1, 0).astype(BF16)


def weight_kernel(meta, own, other, w_out, flat):
    first = meta[M_CORE] == 0
    for i in range(CHIPS):
        a = own[i].astype(F32)
        b = other[i].astype(F32)
        even = jnp.where(first, a, b)
        odd = jnp.where(first, b, a)
        flat[2 * i * SHARD : 2 * i * SHARD + SHARD_PAD] = even
        flat[(2 * i + 1) * SHARD : (2 * i + 1) * SHARD + SHARD_PAD] = odd
    for t in range(N_TP):
        for e in range(2):
            rows = flat[pl.ds(2 * t + e, DH, stride=32)]
            w_out[t, :, e * 128 : (e + 1) * 128] = rows.astype(BF16)


def pieces_of(meta, near, ring):
    y, z = meta[M_Y], meta[M_Z]
    for i in range(NY):
        yield 2 * i + z, lambda i=i: near[i * 384 : (i + 1) * 384]
    for ref, step in ring:
        yield 2 * ((y + step + NY) % NY) + 1 - z, lambda ref=ref: ref[...]


RING = (0, -1, 1, -2, 2, -3, 3, -4)


def weight_grad_kernel(meta, att, near, *refs):
    ring = list(zip(refs[:NY], RING))
    keep, give, cols, flat = refs[NY:]
    att_now = att[...]
    for col, load in pieces_of(meta, near, ring):
        cols[col] = dot(att_now, load(), 0, 0)
    for t in range(N_TP):
        for e in range(2):
            flat[pl.ds(2 * t + e, DH, stride=32)] = cols[t, :, e * 128 : (e + 1) * 128]
    flat[FLAT_ROWS:] = jnp.zeros((flat.shape[0] - FLAT_ROWS, 128), F32)
    first = meta[M_CORE] == 0
    for i in range(CHIPS):
        a = flat[2 * i * SHARD : 2 * i * SHARD + SHARD_PAD]
        b = flat[(2 * i + 1) * SHARD : (2 * i + 1) * SHARD + SHARD_PAD]
        keep[i] = jnp.where(first, a, b)
        give[i] = jnp.where(first, b, a)


def backward_kernel(meta, q, kv, prev, nxt, far, probs, att, w, near, *refs):
    ring = list(zip(refs[:NY], RING))
    dq, dkv, dprev, dnext, dfar, acc = refs[NY:]
    total = jnp.zeros((384, DH), F32)
    for col, load in pieces_of(meta, near, ring):
        total = total + dot(load(), w[col], 1, 1)
    grad_all = total.astype(BF16)
    acc[...] = jnp.zeros(acc.shape, F32)
    dkv[...] = jnp.zeros(dkv.shape, F32)
    scale = DH**-0.5
    for j in range(3):
        rows = slice(j * BLK, (j + 1) * BLK)
        grad = grad_all[rows]
        keys = select(meta, j, 0, kv, prev, nxt, far)
        vals = select(meta, j, 1, kv, prev, nxt, far)
        delta = jnp.sum(grad.astype(F32) * att[rows].astype(F32), axis=-1, keepdims=True)
        p = probs[j]
        ds = (p * (dot(grad, vals, 1, 1) - delta)).astype(BF16)
        dq[rows] = dot(ds, keys, 1, 0) * scale
        parts = (dot(ds, q[rows], 0, 0) * scale, dot(p.astype(BF16), grad, 0, 0))
        for which in range(2):
            part = parts[which]
            dkv[which, rows] += part[:BLK]
            if j == 0:
                dprev[which] = part[BLK : 2 * BLK].astype(BF16)
            else:
                dkv[which, (j - 1) * BLK : j * BLK] += part[BLK : 2 * BLK]
            if j == 2:
                dnext[which] = part[2 * BLK : 3 * BLK].astype(BF16)
            else:
                dkv[which, (j + 1) * BLK : (j + 2) * BLK] += part[2 * BLK : 3 * BLK]
            for k in range(3):
                row = pl.multiple_of(meta[3 * j + k] * BLK, BLK)
                acc[k, which, pl.ds(row, BLK)] += part[(3 + k) * BLK : (4 + k) * BLK]
    dfar[meta[M_X]] = jnp.zeros(dfar.shape[1:], BF16)
    for k in range(3):
        dfar[(meta[M_X] + k + 1) % NX] = acc[k].astype(BF16)


def on_device(queries, key_rows, values, cotangent, w_flat, block_keys):
    ctx = lax.axis_index("ctx")
    tp = lax.axis_index("tp")
    picked = (block_keys[:, 3:] % 3).reshape(9)
    place = jnp.stack([ctx // (2 * NZ), ctx % 2, tp // 2, tp % 2]).astype(jnp.int32)
    meta = jnp.concatenate([picked, place])

    near = lax.all_gather(cotangent, "tp", axis=0, tiled=True, axis_index_groups=Y_GROUPS)
    twin = twin_swap(cotangent)
    kv = jnp.stack([key_rows, values])
    prev = ctx_shift(kv[:, 2 * BLK :], 1)
    nxt = ctx_shift(kv[:, :BLK], -1)
    far = lax.all_to_all(
        jnp.broadcast_to(kv[None], (NX,) + kv.shape),
        "ctx", 0, 0, tiled=True, axis_index_groups=X_GROUPS,
    )
    up, down = twin, twin
    ring = [twin]
    for step in range(1, 4):
        up = y_shift(up, 1)
        down = y_shift(down, -1)
        ring += [up, down]
    ring.append(y_shift(up, 1))

    w_pad = jnp.concatenate([w_flat[0], twin[:2, :128]], axis=0)
    w_own = lax.all_to_all(
        jnp.broadcast_to(w_pad[None], (CHIPS, SHARD_PAD, 128)),
        "ctx", 0, 0, tiled=True, axis_index_groups=SAME_CORE,
    )
    w_other = core_swap(w_own)
    flat_alloc = N_CTX * SHARD + 8
    weight = pl.pallas_call(
        weight_kernel,
        out_shape=jax.ShapeDtypeStruct((N_TP, DH, WCOL), BF16),
        in_specs=[SMEM, VMEM, VMEM],
        out_specs=VMEM,
        scratch_shapes=[pltpu.VMEM((flat_alloc, 128), F32)],
        compiler_params=PARAMS,
        name="weight_rows",
    )(meta, w_own, w_other)

    probs, att = pl.pallas_call(
        forward_kernel,
        out_shape=(
            jax.ShapeDtypeStruct((3, BLK, 6 * BLK), F32),
            jax.ShapeDtypeStruct((384, DH), BF16),
        ),
        in_specs=[SMEM] + [VMEM] * 5,
        out_specs=(VMEM, VMEM),
        compiler_params=PARAMS,
        name="attention_forward",
    )(meta, queries, kv, prev, nxt, far)

    chunk = jax.ShapeDtypeStruct((CHIPS, SHARD_PAD, 128), F32)
    keep, give = pl.pallas_call(
        weight_grad_kernel,
        out_shape=(chunk, chunk),
        in_specs=[SMEM] + [VMEM] * (2 + NY),
        out_specs=(VMEM, VMEM),
        scratch_shapes=[pltpu.VMEM((N_TP, DH, WCOL), F32), pltpu.VMEM((flat_alloc, 128), F32)],
        compiler_params=PARAMS,
        name="weight_grad",
    )(meta, att, near, *ring)
    pair_sum = (keep + core_swap(give)).astype(BF16)
    spread = lax.all_to_all(
        pair_sum, "ctx", 0, 0, tiled=True, axis_index_groups=SAME_CORE
    )
    weight_grad = jnp.sum(spread.astype(F32), axis=0)[None, :SHARD]

    two = (2, 384, DH)
    dq, dkv, dprev, dnext, dfar = pl.pallas_call(
        backward_kernel,
        out_shape=(
            jax.ShapeDtypeStruct((384, DH), F32),
            jax.ShapeDtypeStruct(two, F32),
            jax.ShapeDtypeStruct((2, BLK, DH), BF16),
            jax.ShapeDtypeStruct((2, BLK, DH), BF16),
            jax.ShapeDtypeStruct((NX,) + two, BF16),
        ),
        in_specs=[SMEM] + [VMEM] * (9 + NY),
        out_specs=(VMEM,) * 5,
        scratch_shapes=[pltpu.VMEM((3,) + two, F32)],
        compiler_params=PARAMS,
        name="attention_backward",
    )(meta, queries, kv, prev, nxt, far, probs, att, weight, near, *ring)
    from_far = lax.all_to_all(dfar, "ctx", 0, 0, tiled=True, axis_index_groups=X_GROUPS)
    from_next = ctx_shift(dprev, -1)
    from_prev = ctx_shift(dnext, 1)
    total = dkv + jnp.sum(from_far.astype(F32), axis=0)
    total = total.at[:, 2 * BLK :].add(from_next.astype(F32))
    total = total.at[:, :BLK].add(from_prev.astype(F32))
    return dq, total[0], total[1], weight_grad


def solution(mesh):
    in_specs = (
        P("ctx", "tp"),
        P("ctx", "tp"),
        P("ctx", "tp"),
        P("ctx", "tp"),
        P("tp", "ctx", None),
        P("ctx", None),
    )
    out_specs = (P("ctx", "tp"), P("ctx", "tp"), P("ctx", "tp"), P("tp", "ctx", None))
    return jax.shard_map(
        on_device, mesh=mesh, in_specs=in_specs, out_specs=out_specs, check_vma=False
    )
```

```python
import jax
import jax.numpy as jnp
from jax import lax
from jax.experimental import pallas as pl
from jax.experimental.pallas import tpu as pltpu
from jax.sharding import PartitionSpec as P

DH = 128
BLK = 128
F32 = jnp.float32
BF16 = jnp.bfloat16

NX, NZ, NY = 4, 6, 8
N_CTX = NX * NZ * 2
N_TP = NY * 2
CHIPS = NX * NZ
SHARD = 86
SHARD_PAD = 88
FLAT_ROWS = 4096
WCOL = 256
SAME_CORE = [[2 * i + core for i in range(CHIPS)] for core in range(2)]
X_GROUPS = [[x * NZ * 2 + rest for x in range(NX)] for rest in range(NZ * 2)]
Y_GROUPS = [[2 * y + z for y in range(NY)] for z in range(2)]
SMEM = pl.BlockSpec(memory_space=pltpu.SMEM)
VMEM = pl.BlockSpec(memory_space=pltpu.VMEM)
PARAMS = pltpu.CompilerParams(vmem_limit_bytes=12 * 1024 * 1024)

M_X, M_CORE, M_Y, M_Z = 9, 10, 11, 12


def dot(a, b, ca, cb):
    return lax.dot_general(a, b, (((ca,), (cb,)), ((), ())), preferred_element_type=F32)


def x_shift(value, steps):
    pairs = [(s, (s + steps * NZ * 2) % N_CTX) for s in range(N_CTX)]
    return lax.ppermute(value, "ctx", pairs)


def neighbours(first, last, even):
    inner = core_swap(jnp.where(even, last, first))
    pairs = [(s, (s - 1 if s % 2 == 0 else s + 1) % N_CTX) for s in range(N_CTX)]
    outer = lax.ppermute(jnp.where(even, first, last), "ctx", pairs)
    return jnp.where(even, outer, inner), jnp.where(even, inner, outer)


def core_swap(value):
    return lax.ppermute(value, "ctx", [(s, s ^ 1) for s in range(N_CTX)])


def twin_swap(value):
    return lax.ppermute(value, "tp", [(s, s ^ 1) for s in range(N_TP)])


def y_shift(value, steps):
    pairs = [(2 * y + z, 2 * ((y + steps) % NY) + z) for y in range(NY) for z in range(2)]
    return lax.ppermute(value, "tp", pairs)


def after(value, shards):
    return jnp.where(shards[0, SHARD, 0] == 0, value, jnp.zeros_like(value))


def select(meta, j, which, kv, prev, nxt, far):
    parts = [kv[which, j * BLK : (j + 1) * BLK]]
    parts.append(prev[which] if j == 0 else kv[which, (j - 1) * BLK : j * BLK])
    parts.append(nxt[which] if j == 2 else kv[which, (j + 1) * BLK : (j + 2) * BLK])
    for k in range(3):
        source = (meta[M_X] + k + 1) % NX
        row = pl.multiple_of(meta[3 * j + k] * BLK, BLK)
        parts.append(far[source, which, pl.ds(row, BLK)])
    return jnp.concatenate(parts, axis=0)


def forward_kernel(meta, q, kv, prev, nxt, far, probs_out, att_out):
    for j in range(3):
        rows = slice(j * BLK, (j + 1) * BLK)
        keys = select(meta, j, 0, kv, prev, nxt, far)
        vals = select(meta, j, 1, kv, prev, nxt, far)
        scores = dot(q[rows], keys, 1, 1) * (DH**-0.5)
        terms = jnp.exp(scores - jnp.max(scores, axis=-1, keepdims=True))
        probs = terms / jnp.sum(terms, axis=-1, keepdims=True)
        probs_out[j] = probs
        att_out[rows] = dot(probs.astype(BF16), vals, 1, 0).astype(BF16)


def weight_kernel(meta, own, other, w_out, flat):
    first = meta[M_CORE] == 0
    for i in range(CHIPS):
        a = own[i].astype(F32)
        b = other[i].astype(F32)
        even = jnp.where(first, a, b)
        odd = jnp.where(first, b, a)
        flat[2 * i * SHARD : 2 * i * SHARD + SHARD_PAD] = even
        flat[(2 * i + 1) * SHARD : (2 * i + 1) * SHARD + SHARD_PAD] = odd
    for t in range(N_TP):
        for e in range(2):
            rows = flat[pl.ds(2 * t + e, DH, stride=32)]
            w_out[t, :, e * 128 : (e + 1) * 128] = rows.astype(BF16)


RING = (0, -1, 1, -2, 2, -3, 3, -4)


def cotangent_kernel(meta, w, att, near_hbm, *refs):
    ring = refs[:NY]
    keep, give, grad, near, cols, flat, sem = refs[NY:]
    copy = pltpu.make_async_copy(near_hbm, near, sem)
    copy.start()
    y, z = meta[M_Y], meta[M_Z]
    att_now = att[...]
    total = jnp.zeros((384, DH), F32)
    for piece, step in zip(ring, RING):
        col = 2 * ((y + step + NY) % NY) + 1 - z
        cot = piece[...]
        cols[col] = dot(att_now, cot, 0, 0)
        total = total + dot(cot, w[col], 1, 1)
    copy.wait()
    for i in range(NY):
        col = 2 * i + z
        cot = near[i * 384 : (i + 1) * 384]
        cols[col] = dot(att_now, cot, 0, 0)
        total = total + dot(cot, w[col], 1, 1)
    grad[...] = total.astype(BF16)
    for t in range(N_TP):
        for e in range(2):
            flat[pl.ds(2 * t + e, DH, stride=32)] = cols[t, :, e * 128 : (e + 1) * 128]
    flat[FLAT_ROWS:] = jnp.zeros((flat.shape[0] - FLAT_ROWS, 128), F32)
    first = meta[M_CORE] == 0
    for i in range(CHIPS):
        a = flat[2 * i * SHARD : 2 * i * SHARD + SHARD_PAD]
        b = flat[(2 * i + 1) * SHARD : (2 * i + 1) * SHARD + SHARD_PAD]
        keep[i] = jnp.where(first, a, b)
        give[i] = jnp.where(first, b, a)


def backward_kernel(meta, q, kv, prev, nxt, far, probs, att, out_grad, dq, dkv, dprev, dnext, dfar, acc):
    acc[...] = jnp.zeros(acc.shape, F32)
    dkv[...] = jnp.zeros(dkv.shape, F32)
    scale = DH**-0.5
    for j in range(3):
        rows = slice(j * BLK, (j + 1) * BLK)
        grad = out_grad[rows]
        keys = select(meta, j, 0, kv, prev, nxt, far)
        vals = select(meta, j, 1, kv, prev, nxt, far)
        delta = jnp.sum(grad.astype(F32) * att[rows].astype(F32), axis=-1, keepdims=True)
        p = probs[j]
        ds = (p * (dot(grad, vals, 1, 1) - delta)).astype(BF16)
        dq[rows] = dot(ds, keys, 1, 0) * scale
        parts = (dot(ds, q[rows], 0, 0) * scale, dot(p.astype(BF16), grad, 0, 0))
        for which in range(2):
            part = parts[which]
            dkv[which, rows] += part[:BLK]
            if j == 0:
                dprev[which] = part[BLK : 2 * BLK].astype(BF16)
            else:
                dkv[which, (j - 1) * BLK : j * BLK] += part[BLK : 2 * BLK]
            if j == 2:
                dnext[which] = part[2 * BLK : 3 * BLK].astype(BF16)
            else:
                dkv[which, (j + 1) * BLK : (j + 2) * BLK] += part[2 * BLK : 3 * BLK]
            for k in range(3):
                row = pl.multiple_of(meta[3 * j + k] * BLK, BLK)
                acc[k, which, pl.ds(row, BLK)] += part[(3 + k) * BLK : (4 + k) * BLK]
    dfar[...] = acc[...].astype(BF16)


def chunk_sum_kernel(parts, out):
    total = parts[0].astype(F32)
    for i in range(1, CHIPS):
        total = total + parts[i].astype(F32)
    out[0] = total[:SHARD]


def grad_sum_kernel(dkv, prev, nxt, far1, far2, far3, dk, dv):
    for which, out in ((0, dk), (1, dv)):
        out[...] = (
            dkv[which]
            + far1[which].astype(F32)
            + far2[which].astype(F32)
            + far3[which].astype(F32)
        )
        out[:BLK] += prev[which].astype(F32)
        out[2 * BLK :] += nxt[which].astype(F32)


def on_device(queries, key_rows, values, cotangent, w_flat, block_keys):
    ctx = lax.axis_index("ctx")
    tp = lax.axis_index("tp")
    picked = (block_keys[:, 3:] % 3).reshape(9)
    place = jnp.stack([ctx // (2 * NZ), ctx % 2, tp // 2, tp % 2]).astype(jnp.int32)
    meta = jnp.concatenate([picked, place])

    near = lax.all_gather(cotangent, "tp", axis=0, tiled=True, axis_index_groups=Y_GROUPS)
    twin = twin_swap(cotangent)
    w_pad = jnp.pad(w_flat[0], ((0, SHARD_PAD - SHARD), (0, 0)))
    w_own = lax.all_to_all(
        jnp.broadcast_to(w_pad[None], (CHIPS, SHARD_PAD, 128)),
        "ctx", 0, 0, tiled=True, axis_index_groups=SAME_CORE,
    )
    kv = jnp.stack([key_rows, values])
    even = ctx % 2 == 0
    prev, nxt = neighbours(kv[:, :BLK], kv[:, 2 * BLK :], even)
    far = lax.all_to_all(
        jnp.broadcast_to(after(kv, w_own)[None], (NX,) + kv.shape),
        "ctx", 0, 0, tiled=True, axis_index_groups=X_GROUPS,
    )
    up, down = twin, twin
    ring = [twin]
    for step in range(1, 4):
        up = y_shift(up, 1)
        down = y_shift(down, -1)
        ring += [up, down]
    ring.append(y_shift(up, 1))

    w_other = core_swap(w_own)
    flat_alloc = N_CTX * SHARD + 8
    weight = pl.pallas_call(
        weight_kernel,
        out_shape=jax.ShapeDtypeStruct((N_TP, DH, WCOL), BF16),
        in_specs=[SMEM, VMEM, VMEM],
        out_specs=VMEM,
        scratch_shapes=[pltpu.VMEM((flat_alloc, 128), F32)],
        compiler_params=PARAMS,
        name="weight_rows",
    )(meta, w_own, w_other)

    probs, att = pl.pallas_call(
        forward_kernel,
        out_shape=(
            jax.ShapeDtypeStruct((3, BLK, 6 * BLK), F32),
            jax.ShapeDtypeStruct((384, DH), BF16),
        ),
        in_specs=[SMEM] + [VMEM] * 5,
        out_specs=(VMEM, VMEM),
        compiler_params=PARAMS,
        name="attention_forward",
    )(meta, queries, kv, prev, nxt, far)

    chunk = jax.ShapeDtypeStruct((CHIPS, SHARD_PAD, 128), F32)
    keep, give, out_grad = pl.pallas_call(
        cotangent_kernel,
        out_shape=(chunk, chunk, jax.ShapeDtypeStruct((384, DH), BF16)),
        in_specs=[SMEM, VMEM, VMEM, pl.BlockSpec(memory_space=pltpu.HBM)] + [VMEM] * NY,
        out_specs=(VMEM, VMEM, VMEM),
        scratch_shapes=[
            pltpu.VMEM((NY * 384, WCOL), BF16),
            pltpu.VMEM((N_TP, DH, WCOL), F32),
            pltpu.VMEM((flat_alloc, 128), F32),
            pltpu.SemaphoreType.DMA,
        ],
        compiler_params=PARAMS,
        name="cotangent_products",
    )(meta, weight, att, near, *ring)
    pair_sum = (keep + core_swap(give)).astype(BF16)
    spread = lax.all_to_all(
        pair_sum, "ctx", 0, 0, tiled=True, axis_index_groups=SAME_CORE
    )
    weight_grad = pl.pallas_call(
        chunk_sum_kernel,
        out_shape=jax.ShapeDtypeStruct((1, SHARD, 128), F32),
        compiler_params=PARAMS,
        name="chunk_sum",
    )(spread)

    two = (2, 384, DH)
    dq, dkv, dprev, dnext, dfar = pl.pallas_call(
        backward_kernel,
        out_shape=(
            jax.ShapeDtypeStruct((384, DH), F32),
            jax.ShapeDtypeStruct(two, F32),
            jax.ShapeDtypeStruct((2, BLK, DH), BF16),
            jax.ShapeDtypeStruct((2, BLK, DH), BF16),
            jax.ShapeDtypeStruct((3,) + two, BF16),
        ),
        in_specs=[SMEM] + [VMEM] * 8,
        out_specs=(VMEM,) * 5,
        scratch_shapes=[pltpu.VMEM((3,) + two, F32)],
        compiler_params=PARAMS,
        name="attention_backward",
    )(meta, queries, kv, prev, nxt, far, probs, att, out_grad)
    far_back = [x_shift(dfar[k], k + 1) for k in range(3)]
    from_prev, from_next = neighbours(dprev, dnext, even)
    grad = jax.ShapeDtypeStruct((384, DH), F32)
    dk, dv = pl.pallas_call(
        grad_sum_kernel,
        out_shape=(grad, grad),
        compiler_params=PARAMS,
        name="grad_sum",
    )(dkv, from_prev, from_next, *far_back)
    return dq, dk, dv, weight_grad


def solution(mesh):
    in_specs = (
        P("ctx", "tp"),
        P("ctx", "tp"),
        P("ctx", "tp"),
        P("ctx", "tp"),
        P("tp", "ctx", None),
        P("ctx", None),
    )
    out_specs = (P("ctx", "tp"), P("ctx", "tp"), P("ctx", "tp"), P("tp", "ctx", None))
    return jax.shard_map(
        on_device, mesh=mesh, in_specs=in_specs, out_specs=out_specs, check_vma=False
    )
```

```python
import jax
import jax.numpy as jnp
from jax import lax
from jax.experimental import pallas as pl
from jax.experimental.pallas import tpu as pltpu
from jax.sharding import PartitionSpec as P

DH = 128
BLK = 128
F32 = jnp.float32
BF16 = jnp.bfloat16

NX, NZ, NY = 4, 6, 8
N_CTX = NX * NZ * 2
N_TP = NY * 2
CHIPS = NX * NZ
SHARD = 86
SHARD_PAD = 88
FLAT_ROWS = 4096
WCOL = 256
SAME_CORE = [[2 * i + core for i in range(CHIPS)] for core in range(2)]
X_GROUPS = [[x * NZ * 2 + rest for x in range(NX)] for rest in range(NZ * 2)]
Y_GROUPS = [[2 * y + z for y in range(NY)] for z in range(2)]
SMEM = pl.BlockSpec(memory_space=pltpu.SMEM)
VMEM = pl.BlockSpec(memory_space=pltpu.VMEM)
PARAMS = pltpu.CompilerParams(vmem_limit_bytes=12 * 1024 * 1024)

M_X, M_CORE, M_Y, M_Z = 9, 10, 11, 12


def dot(a, b, ca, cb):
    return lax.dot_general(a, b, (((ca,), (cb,)), ((), ())), preferred_element_type=F32)


def x_shift(value, steps):
    pairs = [(s, (s + steps * NZ * 2) % N_CTX) for s in range(N_CTX)]
    return lax.ppermute(value, "ctx", pairs)


def neighbours(first, last, even):
    inner = core_swap(jnp.where(even, last, first))
    pairs = [(s, (s - 1 if s % 2 == 0 else s + 1) % N_CTX) for s in range(N_CTX)]
    outer = lax.ppermute(jnp.where(even, first, last), "ctx", pairs)
    return jnp.where(even, outer, inner), jnp.where(even, inner, outer)


def core_swap(value):
    return lax.ppermute(value, "ctx", [(s, s ^ 1) for s in range(N_CTX)])


def twin_swap(value):
    return lax.ppermute(value, "tp", [(s, s ^ 1) for s in range(N_TP)])


def after(value, element):
    return jnp.where(element < jnp.inf, value, jnp.zeros_like(value))


def select(meta, j, which, kv, prev, nxt, far):
    parts = [kv[which, j * BLK : (j + 1) * BLK]]
    parts.append(prev[which] if j == 0 else kv[which, (j - 1) * BLK : j * BLK])
    parts.append(nxt[which] if j == 2 else kv[which, (j + 1) * BLK : (j + 2) * BLK])
    for k in range(3):
        source = (meta[M_X] + k + 1) % NX
        row = pl.multiple_of(meta[3 * j + k] * BLK, BLK)
        parts.append(far[source, which, pl.ds(row, BLK)])
    return jnp.concatenate(parts, axis=0)


def forward_kernel(meta, q, kv, prev, nxt, far, probs_out, att_out):
    for j in range(3):
        rows = slice(j * BLK, (j + 1) * BLK)
        keys = select(meta, j, 0, kv, prev, nxt, far)
        vals = select(meta, j, 1, kv, prev, nxt, far)
        scores = dot(q[rows], keys, 1, 1) * (DH**-0.5)
        terms = jnp.exp(scores - jnp.max(scores, axis=-1, keepdims=True))
        probs = terms / jnp.sum(terms, axis=-1, keepdims=True)
        probs_out[j] = probs
        att_out[rows] = dot(probs.astype(BF16), vals, 1, 0).astype(BF16)


def weight_kernel(meta, own, other, w_out, flat):
    first = meta[M_CORE] == 0
    for i in range(CHIPS):
        a = own[i].astype(F32)
        b = other[i].astype(F32)
        even = jnp.where(first, a, b)
        odd = jnp.where(first, b, a)
        flat[2 * i * SHARD : 2 * i * SHARD + SHARD_PAD] = even
        flat[(2 * i + 1) * SHARD : (2 * i + 1) * SHARD + SHARD_PAD] = odd
    for t in range(N_TP):
        for e in range(2):
            rows = flat[pl.ds(2 * t + e, DH, stride=32)]
            w_out[t, :, e * 128 : (e + 1) * 128] = rows.astype(BF16)


def cotangent_kernel(meta, w, att, pieces, keep, give, grad, cols, flat):
    z = meta[M_Z]
    att_now = att[...]
    total = jnp.zeros((384, DH), F32)
    for i in range(N_TP):
        col = 2 * (i // 2) + (z if i % 2 == 0 else 1 - z)
        cot = pieces[i * 384 : (i + 1) * 384]
        cols[col] = dot(att_now, cot, 0, 0)
        total = total + dot(cot, w[col], 1, 1)
    grad[...] = total.astype(BF16)
    for t in range(N_TP):
        for e in range(2):
            flat[pl.ds(2 * t + e, DH, stride=32)] = cols[t, :, e * 128 : (e + 1) * 128]
    flat[FLAT_ROWS:] = jnp.zeros((flat.shape[0] - FLAT_ROWS, 128), F32)
    first = meta[M_CORE] == 0
    for i in range(CHIPS):
        a = flat[2 * i * SHARD : 2 * i * SHARD + SHARD_PAD]
        b = flat[(2 * i + 1) * SHARD : (2 * i + 1) * SHARD + SHARD_PAD]
        keep[i] = jnp.where(first, a, b)
        give[i] = jnp.where(first, b, a)


def backward_kernel(meta, q, kv, prev, nxt, far, probs, att, out_grad, dq, dkv, dprev, dnext, dfar, acc):
    acc[...] = jnp.zeros(acc.shape, F32)
    dkv[...] = jnp.zeros(dkv.shape, F32)
    scale = DH**-0.5
    for j in range(3):
        rows = slice(j * BLK, (j + 1) * BLK)
        grad = out_grad[rows]
        keys = select(meta, j, 0, kv, prev, nxt, far)
        vals = select(meta, j, 1, kv, prev, nxt, far)
        delta = jnp.sum(grad.astype(F32) * att[rows].astype(F32), axis=-1, keepdims=True)
        p = probs[j]
        ds = (p * (dot(grad, vals, 1, 1) - delta)).astype(BF16)
        dq[rows] = dot(ds, keys, 1, 0) * scale
        parts = (dot(ds, q[rows], 0, 0) * scale, dot(p.astype(BF16), grad, 0, 0))
        for which in range(2):
            part = parts[which]
            dkv[which, rows] += part[:BLK]
            if j == 0:
                dprev[which] = part[BLK : 2 * BLK].astype(BF16)
            else:
                dkv[which, (j - 1) * BLK : j * BLK] += part[BLK : 2 * BLK]
            if j == 2:
                dnext[which] = part[2 * BLK : 3 * BLK].astype(BF16)
            else:
                dkv[which, (j + 1) * BLK : (j + 2) * BLK] += part[2 * BLK : 3 * BLK]
            for k in range(3):
                row = pl.multiple_of(meta[3 * j + k] * BLK, BLK)
                acc[k, which, pl.ds(row, BLK)] += part[(3 + k) * BLK : (4 + k) * BLK]
    dfar[...] = acc[...].astype(BF16)


def chunk_sum_kernel(parts, out):
    total = parts[0].astype(F32)
    for i in range(1, CHIPS):
        total = total + parts[i].astype(F32)
    out[0] = total[:SHARD]


def grad_sum_kernel(dkv, prev, nxt, far1, far2, far3, dk, dv):
    for which, out in ((0, dk), (1, dv)):
        out[...] = (
            dkv[which]
            + far1[which].astype(F32)
            + far2[which].astype(F32)
            + far3[which].astype(F32)
        )
        out[:BLK] += prev[which].astype(F32)
        out[2 * BLK :] += nxt[which].astype(F32)


def on_device(queries, key_rows, values, cotangent, w_flat, block_keys):
    ctx = lax.axis_index("ctx")
    tp = lax.axis_index("tp")
    picked = (block_keys[:, 3:] % 3).reshape(9)
    place = jnp.stack([ctx // (2 * NZ), ctx % 2, tp // 2, tp % 2]).astype(jnp.int32)
    meta = jnp.concatenate([picked, place])

    twin = twin_swap(cotangent)
    pieces = lax.all_gather(
        jnp.concatenate([cotangent, twin], axis=0),
        "tp", axis=0, tiled=True, axis_index_groups=Y_GROUPS,
    )
    w_pad = jnp.concatenate([w_flat[0], twin[: SHARD_PAD - SHARD, :128]], axis=0)
    w_own = lax.all_to_all(
        jnp.broadcast_to(w_pad[None], (CHIPS, SHARD_PAD, 128)),
        "ctx", 0, 0, tiled=True, axis_index_groups=SAME_CORE,
    )
    kv = after(jnp.stack([key_rows, values]), twin[0, 0])
    even = ctx % 2 == 0
    prev, nxt = neighbours(kv[:, :BLK], kv[:, 2 * BLK :], even)
    far = lax.all_to_all(
        jnp.broadcast_to(after(kv, w_own[0, 0, 0])[None], (NX,) + kv.shape),
        "ctx", 0, 0, tiled=True, axis_index_groups=X_GROUPS,
    )
    w_other = core_swap(w_own)
    flat_alloc = N_CTX * SHARD + 8
    weight = pl.pallas_call(
        weight_kernel,
        out_shape=jax.ShapeDtypeStruct((N_TP, DH, WCOL), BF16),
        in_specs=[SMEM, VMEM, VMEM],
        out_specs=VMEM,
        scratch_shapes=[pltpu.VMEM((flat_alloc, 128), F32)],
        compiler_params=PARAMS,
        name="weight_rows",
    )(meta, w_own, w_other)

    probs, att = pl.pallas_call(
        forward_kernel,
        out_shape=(
            jax.ShapeDtypeStruct((3, BLK, 6 * BLK), F32),
            jax.ShapeDtypeStruct((384, DH), BF16),
        ),
        in_specs=[SMEM] + [VMEM] * 5,
        out_specs=(VMEM, VMEM),
        compiler_params=PARAMS,
        name="attention_forward",
    )(meta, queries, kv, prev, nxt, far)

    chunk = jax.ShapeDtypeStruct((CHIPS, SHARD_PAD, 128), F32)
    keep, give, out_grad = pl.pallas_call(
        cotangent_kernel,
        out_shape=(chunk, chunk, jax.ShapeDtypeStruct((384, DH), BF16)),
        in_specs=[SMEM, VMEM, VMEM, VMEM],
        out_specs=(VMEM, VMEM, VMEM),
        scratch_shapes=[
            pltpu.VMEM((N_TP, DH, WCOL), F32),
            pltpu.VMEM((flat_alloc, 128), F32),
        ],
        compiler_params=PARAMS,
        name="cotangent_products",
    )(meta, weight, att, pieces)
    pair_sum = (keep + core_swap(give)).astype(BF16)
    spread = lax.all_to_all(
        pair_sum, "ctx", 0, 0, tiled=True, axis_index_groups=SAME_CORE
    )
    weight_grad = pl.pallas_call(
        chunk_sum_kernel,
        out_shape=jax.ShapeDtypeStruct((1, SHARD, 128), F32),
        compiler_params=PARAMS,
        name="chunk_sum",
    )(spread)

    two = (2, 384, DH)
    dq, dkv, dprev, dnext, dfar = pl.pallas_call(
        backward_kernel,
        out_shape=(
            jax.ShapeDtypeStruct((384, DH), F32),
            jax.ShapeDtypeStruct(two, F32),
            jax.ShapeDtypeStruct((2, BLK, DH), BF16),
            jax.ShapeDtypeStruct((2, BLK, DH), BF16),
            jax.ShapeDtypeStruct((3,) + two, BF16),
        ),
        in_specs=[SMEM] + [VMEM] * 8,
        out_specs=(VMEM,) * 5,
        scratch_shapes=[pltpu.VMEM((3,) + two, F32)],
        compiler_params=PARAMS,
        name="attention_backward",
    )(meta, queries, kv, prev, nxt, far, probs, att, out_grad)
    far_back = [x_shift(dfar[k], k + 1) for k in range(3)]
    from_prev, from_next = neighbours(dprev, dnext, even)
    grad = jax.ShapeDtypeStruct((384, DH), F32)
    dk, dv = pl.pallas_call(
        grad_sum_kernel,
        out_shape=(grad, grad),
        compiler_params=PARAMS,
        name="grad_sum",
    )(dkv, from_prev, from_next, *far_back)
    return dq, dk, dv, weight_grad


def solution(mesh):
    in_specs = (
        P("ctx", "tp"),
        P("ctx", "tp"),
        P("ctx", "tp"),
        P("ctx", "tp"),
        P("tp", "ctx", None),
        P("ctx", None),
    )
    out_specs = (P("ctx", "tp"), P("ctx", "tp"), P("ctx", "tp"), P("tp", "ctx", None))
    return jax.shard_map(
        on_device, mesh=mesh, in_specs=in_specs, out_specs=out_specs, check_vma=False
    )
```

```python
import jax
import jax.numpy as jnp
from jax import lax
from jax.experimental import pallas as pl
from jax.experimental.pallas import tpu as pltpu
from jax.sharding import PartitionSpec as P

DH = 128
BLK = 128
F32 = jnp.float32
BF16 = jnp.bfloat16

NX, NZ, NY = 4, 6, 8
N_CTX = NX * NZ * 2
N_TP = NY * 2
CHIPS = NX * NZ
SHARD = 86
SHARD_PAD = 88
FLAT_ROWS = 4096
WCOL = 256
SAME_CORE = [[2 * i + core for i in range(CHIPS)] for core in range(2)]
X_GROUPS = [[x * NZ * 2 + rest for x in range(NX)] for rest in range(NZ * 2)]
Y_GROUPS = [[2 * y + z for y in range(NY)] for z in range(2)]
SMEM = pl.BlockSpec(memory_space=pltpu.SMEM)
VMEM = pl.BlockSpec(memory_space=pltpu.VMEM)
PARAMS = pltpu.CompilerParams(vmem_limit_bytes=12 * 1024 * 1024)

ROW_LSE, ROW_PICKS, SHARE_ROWS = 384, 387, 392

WIDE = 1024

M_X, M_CORE, M_Y, M_Z = 9, 10, 11, 12


def dot(a, b, ca, cb):
    return lax.dot_general(a, b, (((ca,), (cb,)), ((), ())), preferred_element_type=F32)


def x_shift(value, steps):
    pairs = [(s, (s + steps * NZ * 2) % N_CTX) for s in range(N_CTX)]
    return lax.ppermute(value, "ctx", pairs)


def neighbours(first, last, even):
    inner = core_swap(jnp.where(even, last, first))
    pairs = [(s, (s - 1 if s % 2 == 0 else s + 1) % N_CTX) for s in range(N_CTX)]
    outer = lax.ppermute(jnp.where(even, first, last), "ctx", pairs)
    return jnp.where(even, outer, inner), jnp.where(even, inner, outer)


def core_swap(value):
    return lax.ppermute(value, "ctx", [(s, s ^ 1) for s in range(N_CTX)])


def twin_swap(value):
    return lax.ppermute(value, "tp", [(s, s ^ 1) for s in range(N_TP)])


def after(value, element):
    return jnp.where(element < jnp.inf, value, jnp.zeros_like(value))


def select(meta, j, which, kv, prev, nxt, far):
    parts = [kv[which, j * BLK : (j + 1) * BLK]]
    parts.append(prev[which] if j == 0 else kv[which, (j - 1) * BLK : j * BLK])
    parts.append(nxt[which] if j == 2 else kv[which, (j + 1) * BLK : (j + 2) * BLK])
    for k in range(3):
        row = pl.multiple_of(meta[3 * j + k] * BLK, BLK)
        parts.append(far[k][which, pl.ds(row, BLK)])
    return jnp.concatenate(parts, axis=0)


def as_row(column):
    return jnp.broadcast_to(column, (BLK, BLK)).T


def forward_kernel(meta, q, kv, prev, nxt, far1, far2, far3, probs_out, att_out, share):
    far = (far1, far2, far3)
    for j in range(3):
        rows = slice(j * BLK, (j + 1) * BLK)
        keys = select(meta, j, 0, kv, prev, nxt, far)
        vals = select(meta, j, 1, kv, prev, nxt, far)
        scores = dot(q[rows], keys, 1, 1) * (DH**-0.5)
        top = jnp.max(scores, axis=-1, keepdims=True)
        terms = jnp.exp(scores - top)
        total = jnp.sum(terms, axis=-1, keepdims=True)
        probs = terms / total
        probs_out[j] = probs
        att = dot(probs.astype(BF16), vals, 1, 0).astype(BF16)
        att_out[rows] = att
        share[rows] = att.astype(F32)
        share[ROW_LSE + j : ROW_LSE + j + 1] = as_row(top + jnp.log(total))[:1]
    lane = lax.broadcasted_iota(jnp.int32, (1, BLK), 1)
    picks = jnp.zeros((1, BLK), F32)
    for i in range(9):
        picks = jnp.where(lane == i, meta[i].astype(F32), picks)
    share[ROW_PICKS : ROW_PICKS + 1] = picks
    share[ROW_PICKS + 1 :] = jnp.zeros((SHARE_ROWS - ROW_PICKS - 1, BLK), F32)


def weight_kernel(meta, own, other, w_out, flat):
    first = meta[M_CORE] == 0
    for i in range(CHIPS):
        a = own[i].astype(F32)
        b = other[i].astype(F32)
        even = jnp.where(first, a, b)
        odd = jnp.where(first, b, a)
        flat[2 * i * SHARD : 2 * i * SHARD + SHARD_PAD] = even
        flat[(2 * i + 1) * SHARD : (2 * i + 1) * SHARD + SHARD_PAD] = odd
    for t in range(N_TP):
        for e in range(2):
            rows = flat[pl.ds(2 * t + e, DH, stride=32)]
            w_out[t, :, e * 128 : (e + 1) * 128] = rows.astype(BF16)


def cotangent_kernel(meta, far_picks, w, att, pieces, keep, give, grad, wide, cols, flat):
    del far_picks
    z = meta[M_Z]
    att_now = att[...]
    total = jnp.zeros((384, DH), F32)
    for i in range(N_TP):
        col = 2 * (i // 2) + (z if i % 2 == 0 else 1 - z)
        cot = pieces[i * 384 : (i + 1) * 384]
        cols[col] = dot(att_now, cot, 0, 0)
        total = total + dot(cot, w[col], 1, 1)
    grad[...] = total.astype(BF16)
    wide[:384] = total.astype(BF16)
    wide[384:] = jnp.zeros((WIDE - 384, DH), BF16)
    for t in range(N_TP):
        for e in range(2):
            flat[pl.ds(2 * t + e, DH, stride=32)] = cols[t, :, e * 128 : (e + 1) * 128]
    flat[FLAT_ROWS:] = jnp.zeros((flat.shape[0] - FLAT_ROWS, 128), F32)
    first = meta[M_CORE] == 0
    for i in range(CHIPS):
        a = flat[2 * i * SHARD : 2 * i * SHARD + SHARD_PAD]
        b = flat[(2 * i + 1) * SHARD : (2 * i + 1) * SHARD + SHARD_PAD]
        keep[i] = jnp.where(first, a, b)
        give[i] = jnp.where(first, b, a)


def backward_kernel(
    meta, q, kv, prev, nxt, far1, far2, far3, probs, att, out_grad, dq, dkv, dprev, dnext
):
    far = (far1, far2, far3)
    dkv[...] = jnp.zeros(dkv.shape, F32)
    scale = DH**-0.5
    for j in range(3):
        rows = slice(j * BLK, (j + 1) * BLK)
        grad = out_grad[rows]
        keys = select(meta, j, 0, kv, prev, nxt, far)
        vals = select(meta, j, 1, kv, prev, nxt, far)
        delta = jnp.sum(grad.astype(F32) * att[rows].astype(F32), axis=-1, keepdims=True)
        p = probs[j]
        ds = (p * (dot(grad, vals, 1, 1) - delta)).astype(BF16)
        dq[rows] = dot(ds, keys, 1, 0) * scale
        band = slice(0, 3 * BLK)
        parts = (
            dot(ds[:, band], q[rows], 0, 0) * scale,
            dot(p[:, band].astype(BF16), grad, 0, 0),
        )
        for which in range(2):
            part = parts[which]
            dkv[which, rows] += part[:BLK]
            if j == 0:
                dprev[which] = part[BLK : 2 * BLK].astype(BF16)
            else:
                dkv[which, (j - 1) * BLK : j * BLK] += part[BLK : 2 * BLK]
            if j == 2:
                dnext[which] = part[2 * BLK :].astype(BF16)
            else:
                dkv[which, (j + 1) * BLK : (j + 2) * BLK] += part[2 * BLK :]


def far_kernel(meta, far_picks, kv, far1, far2, far3, share, grads, dkv, prev, nxt, dk, dv):
    far = (far1, far2, far3)
    scale = DH**-0.5
    for which, out in ((0, dk), (1, dv)):
        out[...] = dkv[which]
        out[:BLK] += prev[which].astype(F32)
        out[2 * BLK :] += nxt[which].astype(F32)
    for k in range(1, 4):
        source = (meta[M_X] + NX - k) % NX
        for j in range(3):
            row = pl.multiple_of(far_picks[source * 9 + 3 * j + k - 1] * BLK, BLK)
            keys = kv[0, pl.ds(row, BLK)]
            vals = kv[1, pl.ds(row, BLK)]
            q = far[3 - k][2, j * BLK : (j + 1) * BLK]
            grad = grads[pl.ds(pl.multiple_of(source * WIDE + j * BLK, BLK), BLK)]
            att = share[source, j * BLK : (j + 1) * BLK]
            lse = share[source, ROW_LSE + j : ROW_LSE + j + 1]
            probs = jnp.exp(dot(keys, q, 1, 1) * scale - lse)
            delta = as_row(jnp.sum(grad.astype(F32) * att, axis=-1, keepdims=True))
            ds = (probs * (dot(vals, grad, 1, 1) - delta)).astype(BF16)
            dk[pl.ds(row, BLK)] += dot(ds, q, 1, 0) * scale
            dv[pl.ds(row, BLK)] += dot(probs.astype(BF16), grad, 1, 0)


def chunk_sum_kernel(parts, out):
    total = parts[0].astype(F32)
    for i in range(1, CHIPS):
        total = total + parts[i].astype(F32)
    out[0] = total[:SHARD]


def on_device(queries, key_rows, values, cotangent, w_flat, block_keys):
    ctx = lax.axis_index("ctx")
    tp = lax.axis_index("tp")
    picked = (block_keys[:, 3:] % 3).reshape(9)
    place = jnp.stack([ctx // (2 * NZ), ctx % 2, tp // 2, tp % 2]).astype(jnp.int32)
    meta = jnp.concatenate([picked, place])

    twin = twin_swap(cotangent)
    pieces = lax.all_gather(
        jnp.concatenate([cotangent, twin], axis=0),
        "tp", axis=0, tiled=True, axis_index_groups=Y_GROUPS,
    )
    w_pad = jnp.concatenate([w_flat[0], twin[: SHARD_PAD - SHARD, :128]], axis=0)
    w_own = lax.all_to_all(
        jnp.broadcast_to(w_pad[None], (CHIPS, SHARD_PAD, 128)),
        "ctx", 0, 0, tiled=True, axis_index_groups=SAME_CORE,
    )
    kv = after(jnp.stack([key_rows, values]), twin[0, 0])
    even = ctx % 2 == 0
    prev, nxt = neighbours(kv[:, :BLK], kv[:, 2 * BLK :], even)
    kvq = jnp.concatenate([kv, queries[None]], axis=0)
    far = [x_shift(kvq, -k) for k in (1, 2, 3)]
    w_other = core_swap(after(w_own, far[2][0, 0, 0] + prev[0, 0, 0]))
    flat_alloc = N_CTX * SHARD + 8
    weight = pl.pallas_call(
        weight_kernel,
        out_shape=jax.ShapeDtypeStruct((N_TP, DH, WCOL), BF16),
        in_specs=[SMEM, VMEM, VMEM],
        out_specs=VMEM,
        scratch_shapes=[pltpu.VMEM((flat_alloc, 128), F32)],
        compiler_params=PARAMS,
        name="weight_rows",
    )(meta, w_own, w_other)

    probs, att, share = pl.pallas_call(
        forward_kernel,
        out_shape=(
            jax.ShapeDtypeStruct((3, BLK, 6 * BLK), F32),
            jax.ShapeDtypeStruct((384, DH), BF16),
            jax.ShapeDtypeStruct((SHARE_ROWS, DH), F32),
        ),
        in_specs=[SMEM] + [VMEM] * 7,
        out_specs=(VMEM,) * 3,
        compiler_params=PARAMS,
        name="attention_forward",
    )(meta, queries, kv, prev, nxt, *far)
    shares = lax.all_to_all(
        jnp.broadcast_to(share[None], (NX,) + share.shape),
        "ctx", 0, 0, tiled=True, axis_index_groups=X_GROUPS,
    )
    far_picks = shares[:, ROW_PICKS, :9].astype(jnp.int32).reshape(NX * 9)

    chunk = jax.ShapeDtypeStruct((CHIPS, SHARD_PAD, 128), F32)
    keep, give, out_grad, wide_grad = pl.pallas_call(
        cotangent_kernel,
        out_shape=(chunk, chunk, jax.ShapeDtypeStruct((384, DH), BF16), jax.ShapeDtypeStruct((WIDE, DH), BF16)),
        in_specs=[SMEM, SMEM, VMEM, VMEM, VMEM],
        out_specs=(VMEM, VMEM, VMEM, VMEM),
        scratch_shapes=[
            pltpu.VMEM((N_TP, DH, WCOL), F32),
            pltpu.VMEM((flat_alloc, 128), F32),
        ],
        compiler_params=PARAMS,
        name="cotangent_products",
    )(meta, far_picks, weight, att, pieces)
    pair_sum = (keep + core_swap(give)).astype(BF16)
    spread = lax.all_to_all(
        pair_sum, "ctx", 0, 0, tiled=True, axis_index_groups=SAME_CORE
    )
    weight_grad = pl.pallas_call(
        chunk_sum_kernel,
        out_shape=jax.ShapeDtypeStruct((1, SHARD, 128), F32),
        compiler_params=PARAMS,
        name="chunk_sum",
    )(spread)

    grads = lax.all_gather(wide_grad, "ctx", axis=0, tiled=True, axis_index_groups=X_GROUPS)
    dq, dkv, dprev, dnext = pl.pallas_call(
        backward_kernel,
        out_shape=(
            jax.ShapeDtypeStruct((384, DH), F32),
            jax.ShapeDtypeStruct((2, 384, DH), F32),
            jax.ShapeDtypeStruct((2, BLK, DH), BF16),
            jax.ShapeDtypeStruct((2, BLK, DH), BF16),
        ),
        in_specs=[SMEM] + [VMEM] * 10,
        out_specs=(VMEM,) * 4,
        compiler_params=PARAMS,
        name="attention_backward",
    )(meta, queries, kv, prev, nxt, *far, probs, att, out_grad)
    from_prev, from_next = neighbours(dprev, dnext, even)
    grad = jax.ShapeDtypeStruct((384, DH), F32)
    dk, dv = pl.pallas_call(
        far_kernel,
        out_shape=(grad, grad),
        in_specs=[SMEM, SMEM] + [VMEM] * 9,
        out_specs=(VMEM, VMEM),
        compiler_params=PARAMS,
        name="far_gradients",
    )(meta, far_picks, kv, *far, shares, grads, dkv, from_prev, from_next)
    return dq, dk, dv, weight_grad


def solution(mesh):
    in_specs = (
        P("ctx", "tp"),
        P("ctx", "tp"),
        P("ctx", "tp"),
        P("ctx", "tp"),
        P("tp", "ctx", None),
        P("ctx", None),
    )
    out_specs = (P("ctx", "tp"), P("ctx", "tp"), P("ctx", "tp"), P("tp", "ctx", None))
    return jax.shard_map(
        on_device, mesh=mesh, in_specs=in_specs, out_specs=out_specs, check_vma=False
    )
```

```python
import jax
import jax.numpy as jnp
from jax import lax
from jax.experimental import pallas as pl
from jax.experimental.pallas import tpu as pltpu
from jax.sharding import PartitionSpec as P

DH = 128
BLK = 128
F32 = jnp.float32
BF16 = jnp.bfloat16

NX, NZ, NY = 4, 6, 8
N_CTX = NX * NZ * 2
N_TP = NY * 2
CHIPS = NX * NZ
SHARD = 86
SHARD_PAD = 88
FLAT_ROWS = 4096
WCOL = 256
SAME_CORE = [[2 * i + core for i in range(CHIPS)] for core in range(2)]
X_GROUPS = [[x * NZ * 2 + rest for x in range(NX)] for rest in range(NZ * 2)]
Y_GROUPS = [[2 * y + z for y in range(NY)] for z in range(2)]
SMEM = pl.BlockSpec(memory_space=pltpu.SMEM)
VMEM = pl.BlockSpec(memory_space=pltpu.VMEM)
PARAMS = pltpu.CompilerParams(vmem_limit_bytes=12 * 1024 * 1024)

M_X, M_CORE, M_Y, M_Z = 9, 10, 11, 12


def dot(a, b, ca, cb):
    return lax.dot_general(a, b, (((ca,), (cb,)), ((), ())), preferred_element_type=F32)


def x_shift(value, steps):
    pairs = [(s, (s + steps * NZ * 2) % N_CTX) for s in range(N_CTX)]
    return lax.ppermute(value, "ctx", pairs)


def neighbours(first, last, even):
    inner = core_swap(jnp.where(even, last, first))
    pairs = [(s, (s - 1 if s % 2 == 0 else s + 1) % N_CTX) for s in range(N_CTX)]
    outer = lax.ppermute(jnp.where(even, first, last), "ctx", pairs)
    return jnp.where(even, outer, inner), jnp.where(even, inner, outer)


def core_swap(value):
    return lax.ppermute(value, "ctx", [(s, s ^ 1) for s in range(N_CTX)])


def twin_swap(value):
    return lax.ppermute(value, "tp", [(s, s ^ 1) for s in range(N_TP)])


def after(value, element):
    return jnp.where(element < jnp.inf, value, jnp.zeros_like(value))


def select(meta, j, which, kv, prev, nxt, far):
    parts = [kv[which, j * BLK : (j + 1) * BLK]]
    parts.append(prev[which] if j == 0 else kv[which, (j - 1) * BLK : j * BLK])
    parts.append(nxt[which] if j == 2 else kv[which, (j + 1) * BLK : (j + 2) * BLK])
    for k in range(3):
        row = pl.multiple_of(meta[3 * j + k] * BLK, BLK)
        parts.append(far[k][which, pl.ds(row, BLK)])
    return jnp.concatenate(parts, axis=0)


def forward_kernel(meta, q, kv, prev, nxt, far1, far2, far3, probs_out, att_out):
    far = (far1, far2, far3)
    for j in range(3):
        rows = slice(j * BLK, (j + 1) * BLK)
        keys = select(meta, j, 0, kv, prev, nxt, far)
        vals = select(meta, j, 1, kv, prev, nxt, far)
        scores = dot(q[rows], keys, 1, 1) * (DH**-0.5)
        terms = jnp.exp(scores - jnp.max(scores, axis=-1, keepdims=True))
        probs = terms / jnp.sum(terms, axis=-1, keepdims=True)
        probs_out[j] = probs
        att_out[rows] = dot(probs.astype(BF16), vals, 1, 0).astype(BF16)


def weight_kernel(meta, own, other, w_out, flat):
    first = meta[M_CORE] == 0
    for i in range(CHIPS):
        a = own[i].astype(F32)
        b = other[i].astype(F32)
        even = jnp.where(first, a, b)
        odd = jnp.where(first, b, a)
        flat[2 * i * SHARD : 2 * i * SHARD + SHARD_PAD] = even
        flat[(2 * i + 1) * SHARD : (2 * i + 1) * SHARD + SHARD_PAD] = odd
    for t in range(N_TP):
        for e in range(2):
            rows = flat[pl.ds(2 * t + e, DH, stride=32)]
            w_out[t, :, e * 128 : (e + 1) * 128] = rows.astype(BF16)


def cotangent_kernel(meta, w, att, pieces, keep, give, grad, cols, flat):
    z = meta[M_Z]
    att_now = att[...]
    total = jnp.zeros((384, DH), F32)
    for i in range(N_TP):
        col = 2 * (i // 2) + (z if i % 2 == 0 else 1 - z)
        cot = pieces[i * 384 : (i + 1) * 384]
        cols[col] = dot(att_now, cot, 0, 0)
        total = total + dot(cot, w[col], 1, 1)
    grad[...] = total.astype(BF16)
    for t in range(N_TP):
        for e in range(2):
            flat[pl.ds(2 * t + e, DH, stride=32)] = cols[t, :, e * 128 : (e + 1) * 128]
    flat[FLAT_ROWS:] = jnp.zeros((flat.shape[0] - FLAT_ROWS, 128), F32)
    first = meta[M_CORE] == 0
    for i in range(CHIPS):
        a = flat[2 * i * SHARD : 2 * i * SHARD + SHARD_PAD]
        b = flat[(2 * i + 1) * SHARD : (2 * i + 1) * SHARD + SHARD_PAD]
        keep[i] = jnp.where(first, a, b)
        give[i] = jnp.where(first, b, a)


def backward_kernel(
    meta, q, kv, prev, nxt, far1, far2, far3, probs, att, out_grad,
    dq, dkv, dprev, dnext, dfar, acc,
):
    far = (far1, far2, far3)
    acc[...] = jnp.zeros(acc.shape, F32)
    dkv[...] = jnp.zeros(dkv.shape, F32)
    scale = DH**-0.5
    for j in range(3):
        rows = slice(j * BLK, (j + 1) * BLK)
        grad = out_grad[rows]
        keys = select(meta, j, 0, kv, prev, nxt, far)
        vals = select(meta, j, 1, kv, prev, nxt, far)
        delta = jnp.sum(grad.astype(F32) * att[rows].astype(F32), axis=-1, keepdims=True)
        p = probs[j]
        ds = (p * (dot(grad, vals, 1, 1) - delta)).astype(BF16)
        dq[rows] = dot(ds, keys, 1, 0) * scale
        parts = (dot(ds, q[rows], 0, 0) * scale, dot(p.astype(BF16), grad, 0, 0))
        for which in range(2):
            part = parts[which]
            dkv[which, rows] += part[:BLK]
            if j == 0:
                dprev[which] = part[BLK : 2 * BLK].astype(BF16)
            else:
                dkv[which, (j - 1) * BLK : j * BLK] += part[BLK : 2 * BLK]
            if j == 2:
                dnext[which] = part[2 * BLK : 3 * BLK].astype(BF16)
            else:
                dkv[which, (j + 1) * BLK : (j + 2) * BLK] += part[2 * BLK : 3 * BLK]
            for k in range(3):
                row = pl.multiple_of(meta[3 * j + k] * BLK, BLK)
                acc[k, which, pl.ds(row, BLK)] += part[(3 + k) * BLK : (4 + k) * BLK]
    dfar[...] = acc[...].astype(BF16)


def pair_sum_kernel(keep, other, dkv, out):
    del dkv
    out[...] = (keep[...] + other[...]).astype(BF16)


def chunk_sum_kernel(parts, out):
    total = parts[0].astype(F32)
    for i in range(1, CHIPS):
        total = total + parts[i].astype(F32)
    out[0] = total[:SHARD]


def grad_sum_kernel(dkv, prev, nxt, far1, far2, far3, dk, dv):
    for which, out in ((0, dk), (1, dv)):
        out[...] = (
            dkv[which]
            + far1[which].astype(F32)
            + far2[which].astype(F32)
            + far3[which].astype(F32)
        )
        out[:BLK] += prev[which].astype(F32)
        out[2 * BLK :] += nxt[which].astype(F32)


def on_device(queries, key_rows, values, cotangent, w_flat, block_keys):
    ctx = lax.axis_index("ctx")
    tp = lax.axis_index("tp")
    picked = (block_keys[:, 3:] % 3).reshape(9)
    place = jnp.stack([ctx // (2 * NZ), ctx % 2, tp // 2, tp % 2]).astype(jnp.int32)
    meta = jnp.concatenate([picked, place])

    twin = twin_swap(cotangent)
    pieces = lax.all_gather(
        jnp.concatenate([cotangent, twin], axis=0),
        "tp", axis=0, tiled=True, axis_index_groups=Y_GROUPS,
    )
    w_pad = jnp.concatenate([w_flat[0], twin[: SHARD_PAD - SHARD, :128]], axis=0)
    w_own = lax.all_to_all(
        jnp.broadcast_to(w_pad[None], (CHIPS, SHARD_PAD, 128)),
        "ctx", 0, 0, tiled=True, axis_index_groups=SAME_CORE,
    )
    kv = after(jnp.stack([key_rows, values]), twin[0, 0])
    even = ctx % 2 == 0
    prev, nxt = neighbours(kv[:, :BLK], kv[:, 2 * BLK :], even)
    far = [x_shift(kv, -k) for k in (1, 2, 3)]
    arrived = [piece[0, 0, 0] for piece in (prev, nxt, *far)]
    w_other = core_swap(after(w_own, sum(arrived)))
    flat_alloc = N_CTX * SHARD + 8
    weight = pl.pallas_call(
        weight_kernel,
        out_shape=jax.ShapeDtypeStruct((N_TP, DH, WCOL), BF16),
        in_specs=[SMEM, VMEM, VMEM],
        out_specs=VMEM,
        scratch_shapes=[pltpu.VMEM((flat_alloc, 128), F32)],
        compiler_params=PARAMS,
        name="weight_rows",
    )(meta, w_own, w_other)

    probs, att = pl.pallas_call(
        forward_kernel,
        out_shape=(
            jax.ShapeDtypeStruct((3, BLK, 6 * BLK), F32),
            jax.ShapeDtypeStruct((384, DH), BF16),
        ),
        in_specs=[SMEM] + [VMEM] * 7,
        out_specs=(VMEM, VMEM),
        compiler_params=PARAMS,
        name="attention_forward",
    )(meta, queries, kv, prev, nxt, *far)

    chunk = jax.ShapeDtypeStruct((CHIPS, SHARD_PAD, 128), F32)
    keep, give, out_grad = pl.pallas_call(
        cotangent_kernel,
        out_shape=(chunk, chunk, jax.ShapeDtypeStruct((384, DH), BF16)),
        in_specs=[SMEM, VMEM, VMEM, VMEM],
        out_specs=(VMEM, VMEM, VMEM),
        scratch_shapes=[
            pltpu.VMEM((N_TP, DH, WCOL), F32),
            pltpu.VMEM((flat_alloc, 128), F32),
        ],
        compiler_params=PARAMS,
        name="cotangent_products",
    )(meta, weight, att, pieces)
    two = (2, 384, DH)
    dq, dkv, dprev, dnext, dfar = pl.pallas_call(
        backward_kernel,
        out_shape=(
            jax.ShapeDtypeStruct((384, DH), F32),
            jax.ShapeDtypeStruct(two, F32),
            jax.ShapeDtypeStruct((2, BLK, DH), BF16),
            jax.ShapeDtypeStruct((2, BLK, DH), BF16),
            jax.ShapeDtypeStruct((3,) + two, BF16),
        ),
        in_specs=[SMEM] + [VMEM] * 10,
        out_specs=(VMEM,) * 5,
        scratch_shapes=[pltpu.VMEM((3,) + two, F32)],
        compiler_params=PARAMS,
        name="attention_backward",
    )(meta, queries, kv, prev, nxt, *far, probs, att, out_grad)
    pair_sum = pl.pallas_call(
        pair_sum_kernel,
        out_shape=jax.ShapeDtypeStruct((CHIPS, SHARD_PAD, 128), BF16),
        in_specs=[VMEM, VMEM, pl.BlockSpec(memory_space=pl.ANY)],
        out_specs=VMEM,
        compiler_params=PARAMS,
        name="pair_sum",
    )(keep, core_swap(give), dkv)
    spread = lax.all_to_all(
        pair_sum, "ctx", 0, 0, tiled=True, axis_index_groups=SAME_CORE
    )
    weight_grad = pl.pallas_call(
        chunk_sum_kernel,
        out_shape=jax.ShapeDtypeStruct((1, SHARD, 128), F32),
        compiler_params=PARAMS,
        name="chunk_sum",
    )(spread)

    far_back = [x_shift(dfar[k], k + 1) for k in range(3)]
    from_prev, from_next = neighbours(dprev, dnext, even)
    grad = jax.ShapeDtypeStruct((384, DH), F32)
    dk, dv = pl.pallas_call(
        grad_sum_kernel,
        out_shape=(grad, grad),
        compiler_params=PARAMS,
        name="grad_sum",
    )(dkv, from_prev, from_next, *far_back)
    return dq, dk, dv, weight_grad


def solution(mesh):
    in_specs = (
        P("ctx", "tp"),
        P("ctx", "tp"),
        P("ctx", "tp"),
        P("ctx", "tp"),
        P("tp", "ctx", None),
        P("ctx", None),
    )
    out_specs = (P("ctx", "tp"), P("ctx", "tp"), P("ctx", "tp"), P("tp", "ctx", None))
    return jax.shard_map(
        on_device, mesh=mesh, in_specs=in_specs, out_specs=out_specs, check_vma=False
    )
```

```python
import jax
import jax.numpy as jnp
from jax import lax
from jax.experimental import pallas as pl
from jax.experimental.pallas import tpu as pltpu
from jax.sharding import PartitionSpec as P

DH = 128
BLK = 128
F32 = jnp.float32
BF16 = jnp.bfloat16

NX, NZ, NY = 4, 6, 8
N_CTX = NX * NZ * 2
N_TP = NY * 2
CHIPS = NX * NZ
SHARD = 86
SHARD_PAD = 88
FLAT_ROWS = 4096
WCOL = 256
SAME_CORE = [[2 * i + core for i in range(CHIPS)] for core in range(2)]
X_GROUPS = [[x * NZ * 2 + rest for x in range(NX)] for rest in range(NZ * 2)]
Y_GROUPS = [[2 * y + z for y in range(NY)] for z in range(2)]
SMEM = pl.BlockSpec(memory_space=pltpu.SMEM)
VMEM = pl.BlockSpec(memory_space=pltpu.VMEM)
ANY = pl.BlockSpec(memory_space=pl.ANY)
PARAMS = pltpu.CompilerParams(vmem_limit_bytes=12 * 1024 * 1024)

M_X, M_CORE, M_Y, M_Z = 9, 10, 11, 12


def dot(a, b, ca, cb):
    return lax.dot_general(a, b, (((ca,), (cb,)), ((), ())), preferred_element_type=F32)


def x_shift(value, steps):
    pairs = [(s, (s + steps * NZ * 2) % N_CTX) for s in range(N_CTX)]
    return lax.ppermute(value, "ctx", pairs)


def outer_swap(value):
    pairs = [(s, (s - 1 if s % 2 == 0 else s + 1) % N_CTX) for s in range(N_CTX)]
    return lax.ppermute(value, "ctx", pairs)


def neighbours(first, last, even):
    inner = core_swap(jnp.where(even, last, first))
    outer = outer_swap(jnp.where(even, first, last))
    return jnp.where(even, outer, inner), jnp.where(even, inner, outer)


def core_swap(value):
    return lax.ppermute(value, "ctx", [(s, s ^ 1) for s in range(N_CTX)])


def twin_swap(value):
    return lax.ppermute(value, "tp", [(s, s ^ 1) for s in range(N_TP)])


def after(value, element):
    return jnp.where(element < jnp.inf, value, jnp.zeros_like(value))


def select(meta, j, which, kv, prev, nxt, far):
    parts = [kv[which, j * BLK : (j + 1) * BLK]]
    parts.append(prev[which] if j == 0 else kv[which, (j - 1) * BLK : j * BLK])
    parts.append(nxt[which] if j == 2 else kv[which, (j + 1) * BLK : (j + 2) * BLK])
    for k in range(3):
        row = pl.multiple_of(meta[3 * j + k] * BLK, BLK)
        parts.append(far[k][which, pl.ds(row, BLK)])
    return jnp.concatenate(parts, axis=0)


def forward_kernel(meta, q, kv, prev, nxt, far1, far2, far3, probs_out, att_out):
    far = (far1, far2, far3)
    for j in range(3):
        rows = slice(j * BLK, (j + 1) * BLK)
        keys = select(meta, j, 0, kv, prev, nxt, far)
        vals = select(meta, j, 1, kv, prev, nxt, far)
        scores = dot(q[rows], keys, 1, 1) * (DH**-0.5)
        terms = jnp.exp(scores - jnp.max(scores, axis=-1, keepdims=True))
        probs = terms / jnp.sum(terms, axis=-1, keepdims=True)
        probs_out[j] = probs
        att_out[rows] = dot(probs.astype(BF16), vals, 1, 0).astype(BF16)


def join_kernel(own, twin, out, sems):
    copies = [
        pltpu.make_async_copy(own, out.at[:384], sems.at[0]),
        pltpu.make_async_copy(twin, out.at[384:], sems.at[1]),
    ]
    for copy in copies:
        copy.start()
    for copy in copies:
        copy.wait()


def weight_kernel(meta, own, other, w_out, flat):
    first = meta[M_CORE] == 0
    for i in range(CHIPS):
        a = own[i].astype(F32)
        b = other[i].astype(F32)
        even = jnp.where(first, a, b)
        odd = jnp.where(first, b, a)
        flat[2 * i * SHARD : 2 * i * SHARD + SHARD_PAD] = even
        flat[(2 * i + 1) * SHARD : (2 * i + 1) * SHARD + SHARD_PAD] = odd
    for t in range(N_TP):
        for e in range(2):
            rows = flat[pl.ds(2 * t + e, DH, stride=32)]
            w_out[t, :, e * 128 : (e + 1) * 128] = rows.astype(BF16)


def cotangent_kernel(w, att_any, pieces_any, keep, give, grad, att, pieces, cols, flat, sems):
    copies = [pltpu.make_async_copy(att_any, att, sems.at[N_TP])]
    for i in range(N_TP):
        rows = slice(i * 384, (i + 1) * 384)
        copies.append(pltpu.make_async_copy(pieces_any.at[rows], pieces.at[rows], sems.at[i]))
    for copy in copies:
        copy.start()
    z = lax.axis_index("tp") % 2
    copies[0].wait()
    att_now = att[...]
    total = jnp.zeros((384, DH), F32)
    for i in range(N_TP):
        col = 2 * (i // 2) + (z if i % 2 == 0 else 1 - z)
        copies[i + 1].wait()
        cot = pieces[i * 384 : (i + 1) * 384]
        cols[col] = dot(att_now, cot, 0, 0)
        total = total + dot(cot, w[col], 1, 1)
    grad[...] = total.astype(BF16)
    for t in range(N_TP):
        for e in range(2):
            flat[pl.ds(2 * t + e, DH, stride=32)] = cols[t, :, e * 128 : (e + 1) * 128]
    flat[FLAT_ROWS:] = jnp.zeros((flat.shape[0] - FLAT_ROWS, 128), F32)
    first = lax.axis_index("ctx") % 2 == 0
    for i in range(CHIPS):
        a = flat[2 * i * SHARD : 2 * i * SHARD + SHARD_PAD]
        b = flat[(2 * i + 1) * SHARD : (2 * i + 1) * SHARD + SHARD_PAD]
        keep[i] = jnp.where(first, a, b)
        give[i] = jnp.where(first, b, a)


def backward_kernel(
    meta, q, kv, prev, nxt, far1, far2, far3, probs, att, out_grad,
    dq, dkv, inner, outer, dfar1, dfar2, dfar3, acc,
):
    far = (far1, far2, far3)
    even = lax.axis_index("ctx") % 2 == 0
    acc[...] = jnp.zeros(acc.shape, F32)
    dkv[...] = jnp.zeros(dkv.shape, F32)
    scale = DH**-0.5
    to_prev = []
    for j in range(3):
        rows = slice(j * BLK, (j + 1) * BLK)
        grad = out_grad[rows]
        keys = select(meta, j, 0, kv, prev, nxt, far)
        vals = select(meta, j, 1, kv, prev, nxt, far)
        delta = jnp.sum(grad.astype(F32) * att[rows].astype(F32), axis=-1, keepdims=True)
        p = probs[j]
        ds = (p * (dot(grad, vals, 1, 1) - delta)).astype(BF16)
        dq[rows] = dot(ds, keys, 1, 0) * scale
        parts = (dot(ds, q[rows], 0, 0) * scale, dot(p.astype(BF16), grad, 0, 0))
        for which in range(2):
            part = parts[which]
            dkv[which, rows] += part[:BLK]
            if j == 0:
                to_prev.append(part[BLK : 2 * BLK])
            else:
                dkv[which, (j - 1) * BLK : j * BLK] += part[BLK : 2 * BLK]
            if j == 2:
                to_next = part[2 * BLK : 3 * BLK]
                inner[which] = jnp.where(even, to_next, to_prev[which]).astype(BF16)
                outer[which] = jnp.where(even, to_prev[which], to_next).astype(BF16)
            else:
                dkv[which, (j + 1) * BLK : (j + 2) * BLK] += part[2 * BLK : 3 * BLK]
            for k in range(3):
                row = pl.multiple_of(meta[3 * j + k] * BLK, BLK)
                acc[k, which, pl.ds(row, BLK)] += part[(3 + k) * BLK : (4 + k) * BLK]
    for k, out in enumerate((dfar1, dfar2, dfar3)):
        out[...] = acc[k].astype(BF16)


def pair_sum_kernel(keep, other, dkv, out):
    del dkv
    out[...] = (keep[...] + other[...]).astype(BF16)


def chunk_sum_kernel(parts, out):
    total = parts[0].astype(F32)
    for i in range(1, CHIPS):
        total = total + parts[i].astype(F32)
    out[0] = total[:SHARD]


def far_sum_kernel(dkv, far1, far2, far3, out):
    parts = [far[...].astype(F32) for far in (far1, far2, far3)]
    out[...] = dkv[...] + parts[0] + parts[1] + parts[2]


def band_sum_kernel(total, inner, outer, dk, dv):
    even = lax.axis_index("ctx") % 2 == 0
    for which, out in ((0, dk), (1, dv)):
        near, away = inner[which].astype(F32), outer[which].astype(F32)
        out[...] = total[which]
        out[:BLK] += jnp.where(even, away, near)
        out[2 * BLK :] += jnp.where(even, near, away)


def on_device(queries, key_rows, values, cotangent, w_flat, block_keys):
    ctx = lax.axis_index("ctx")
    tp = lax.axis_index("tp")
    picked = (block_keys[:, 3:] % 3).reshape(9)
    place = jnp.stack([ctx // (2 * NZ), ctx % 2, tp // 2, tp % 2]).astype(jnp.int32)
    meta = jnp.concatenate([picked, place])

    twin = twin_swap(cotangent)
    joined = pl.pallas_call(
        join_kernel,
        out_shape=jax.ShapeDtypeStruct((2 * 384, WCOL), BF16),
        in_specs=[ANY, ANY],
        out_specs=ANY,
        scratch_shapes=[pltpu.SemaphoreType.DMA((2,))],
        name="join_pieces",
    )(cotangent, twin)
    pieces = lax.all_gather(
        joined,
        "tp", axis=0, tiled=True, axis_index_groups=Y_GROUPS,
    )
    w_pad = jnp.concatenate([w_flat[0], twin[: SHARD_PAD - SHARD, :128]], axis=0)
    w_own = lax.all_to_all(
        jnp.broadcast_to(w_pad[None], (CHIPS, SHARD_PAD, 128)),
        "ctx", 0, 0, tiled=True, axis_index_groups=SAME_CORE,
    )
    kv = after(jnp.stack([key_rows, values]), twin[0, 0])
    even = ctx % 2 == 0
    prev, nxt = neighbours(kv[:, :BLK], kv[:, 2 * BLK :], even)
    far = [x_shift(kv, -k) for k in (1, 2, 3)]
    arrived = [piece[0, 0, 0] for piece in (prev, nxt, *far)]
    w_other = core_swap(after(w_own, sum(arrived)))
    flat_alloc = N_CTX * SHARD + 8
    weight = pl.pallas_call(
        weight_kernel,
        out_shape=jax.ShapeDtypeStruct((N_TP, DH, WCOL), BF16),
        in_specs=[SMEM, VMEM, VMEM],
        out_specs=VMEM,
        scratch_shapes=[pltpu.VMEM((flat_alloc, 128), F32)],
        compiler_params=PARAMS,
        name="weight_rows",
    )(meta, w_own, w_other)

    probs, att = pl.pallas_call(
        forward_kernel,
        out_shape=(
            jax.ShapeDtypeStruct((3, BLK, 6 * BLK), F32),
            jax.ShapeDtypeStruct((384, DH), BF16),
        ),
        in_specs=[SMEM] + [VMEM] * 7,
        out_specs=(VMEM, VMEM),
        compiler_params=PARAMS,
        name="attention_forward",
    )(meta, queries, kv, prev, nxt, *far)

    chunk = jax.ShapeDtypeStruct((CHIPS, SHARD_PAD, 128), F32)
    keep, give, out_grad = pl.pallas_call(
        cotangent_kernel,
        out_shape=(chunk, chunk, jax.ShapeDtypeStruct((384, DH), BF16)),
        in_specs=[VMEM, ANY, ANY],
        out_specs=(VMEM, VMEM, VMEM),
        scratch_shapes=[
            pltpu.VMEM((384, DH), BF16),
            pltpu.VMEM((N_TP * 384, WCOL), BF16),
            pltpu.VMEM((N_TP, DH, WCOL), F32),
            pltpu.VMEM((flat_alloc, 128), F32),
            pltpu.SemaphoreType.DMA((N_TP + 1,)),
        ],
        compiler_params=pltpu.CompilerParams(vmem_limit_bytes=52 * 1024 * 1024),
        name="cotangent_products",
    )(weight, att, pieces)
    two = (2, 384, DH)
    dq, dkv, inner, outer, *dfar = pl.pallas_call(
        backward_kernel,
        out_shape=(
            jax.ShapeDtypeStruct((384, DH), F32),
            jax.ShapeDtypeStruct(two, F32),
            jax.ShapeDtypeStruct((2, BLK, DH), BF16),
            jax.ShapeDtypeStruct((2, BLK, DH), BF16),
        )
        + (jax.ShapeDtypeStruct(two, BF16),) * 3,
        in_specs=[SMEM] + [VMEM] * 10,
        out_specs=(VMEM,) * 7,
        scratch_shapes=[pltpu.VMEM((3,) + two, F32)],
        compiler_params=PARAMS,
        name="attention_backward",
    )(meta, queries, kv, prev, nxt, *far, probs, att, out_grad)
    pair_sum = pl.pallas_call(
        pair_sum_kernel,
        out_shape=jax.ShapeDtypeStruct((CHIPS, SHARD_PAD, 128), BF16),
        in_specs=[VMEM, VMEM, ANY],
        out_specs=VMEM,
        compiler_params=PARAMS,
        name="pair_sum",
    )(keep, core_swap(give), dkv)
    spread = lax.all_to_all(
        pair_sum, "ctx", 0, 0, tiled=True, axis_index_groups=SAME_CORE
    )
    weight_grad = pl.pallas_call(
        chunk_sum_kernel,
        out_shape=jax.ShapeDtypeStruct((1, SHARD, 128), F32),
        compiler_params=PARAMS,
        name="chunk_sum",
    )(spread)

    far_back = [x_shift(dfar[k], k + 1) for k in range(3)]
    total = pl.pallas_call(
        far_sum_kernel,
        out_shape=jax.ShapeDtypeStruct(two, F32),
        compiler_params=PARAMS,
        name="far_sum",
    )(dkv, *far_back)
    grad = jax.ShapeDtypeStruct((384, DH), F32)
    dk, dv = pl.pallas_call(
        band_sum_kernel,
        out_shape=(grad, grad),
        compiler_params=PARAMS,
        name="band_sum",
    )(total, core_swap(inner), outer_swap(outer))
    return dq, dk, dv, weight_grad


def solution(mesh):
    in_specs = (
        P("ctx", "tp"),
        P("ctx", "tp"),
        P("ctx", "tp"),
        P("ctx", "tp"),
        P("tp", "ctx", None),
        P("ctx", None),
    )
    out_specs = (P("ctx", "tp"), P("ctx", "tp"), P("ctx", "tp"), P("tp", "ctx", None))
    return jax.shard_map(
        on_device, mesh=mesh, in_specs=in_specs, out_specs=out_specs, check_vma=False
    )
```

```python
import jax
import jax.numpy as jnp
from jax import lax
from jax.experimental import pallas as pl
from jax.experimental.pallas import tpu as pltpu
from jax.sharding import PartitionSpec as P

DH = 128
BLK = 128
F32 = jnp.float32
BF16 = jnp.bfloat16

NX, NZ, NY = 4, 6, 8
N_CTX = NX * NZ * 2
N_TP = NY * 2
CHIPS = NX * NZ
SHARD = 86
SHARD_PAD = 88
FLAT_ROWS = 4096
WCOL = 256
SAME_CORE = [[2 * i + core for i in range(CHIPS)] for core in range(2)]
X_GROUPS = [[x * NZ * 2 + rest for x in range(NX)] for rest in range(NZ * 2)]
Z_GROUPS = [
    [(x * NZ + z) * 2 + core for z in range(NZ)] for x in range(NX) for core in range(2)
]
X_FAR = NZ * SHARD_PAD
X_ROWS = X_FAR + 2 * 384
Y_GROUPS = [[2 * y + z for y in range(NY)] for z in range(2)]
SMEM = pl.BlockSpec(memory_space=pltpu.SMEM)
VMEM = pl.BlockSpec(memory_space=pltpu.VMEM)
ANY = pl.BlockSpec(memory_space=pl.ANY)
PARAMS = pltpu.CompilerParams(vmem_limit_bytes=12 * 1024 * 1024)

M_X, M_CORE, M_Y, M_Z = 9, 10, 11, 12


def dot(a, b, ca, cb):
    return lax.dot_general(a, b, (((ca,), (cb,)), ((), ())), preferred_element_type=F32)


def x_shift(value, steps):
    pairs = [(s, (s + steps * NZ * 2) % N_CTX) for s in range(N_CTX)]
    return lax.ppermute(value, "ctx", pairs)


def outer_swap(value):
    pairs = [(s, (s - 1 if s % 2 == 0 else s + 1) % N_CTX) for s in range(N_CTX)]
    return lax.ppermute(value, "ctx", pairs)


def neighbours(first, last, even):
    inner = core_swap(jnp.where(even, last, first))
    outer = outer_swap(jnp.where(even, first, last))
    return jnp.where(even, outer, inner), jnp.where(even, inner, outer)


def core_swap(value):
    return lax.ppermute(value, "ctx", [(s, s ^ 1) for s in range(N_CTX)])


def twin_swap(value):
    return lax.ppermute(value, "tp", [(s, s ^ 1) for s in range(N_TP)])


def after(value, element):
    return jnp.where(element < jnp.inf, value, jnp.zeros_like(value))


def select(meta, j, which, kv, prev, nxt, far):
    parts = [kv[which, j * BLK : (j + 1) * BLK]]
    parts.append(prev[which] if j == 0 else kv[which, (j - 1) * BLK : j * BLK])
    parts.append(nxt[which] if j == 2 else kv[which, (j + 1) * BLK : (j + 2) * BLK])
    for k in range(3):
        row = pl.multiple_of(meta[3 * j + k] * BLK, BLK)
        parts.append(far[k][which, pl.ds(row, BLK)])
    return jnp.concatenate(parts, axis=0)


def forward_kernel(meta, w, q, kv, prev, nxt, far1, far2, far3, probs_out, att_out):
    del w
    far = (far1, far2, far3)
    for j in range(3):
        rows = slice(j * BLK, (j + 1) * BLK)
        keys = select(meta, j, 0, kv, prev, nxt, far)
        vals = select(meta, j, 1, kv, prev, nxt, far)
        scores = dot(q[rows], keys, 1, 1) * (DH**-0.5)
        terms = jnp.exp(scores - jnp.max(scores, axis=-1, keepdims=True))
        probs = terms / jnp.sum(terms, axis=-1, keepdims=True)
        probs_out[j] = probs
        att_out[rows] = dot(probs.astype(BF16), vals, 1, 0).astype(BF16)


def weight_kernel(meta, own, other, w_out, flat):
    first = meta[M_CORE] == 0
    for i in range(CHIPS):
        a = own[i].astype(F32)
        b = other[i].astype(F32)
        even = jnp.where(first, a, b)
        odd = jnp.where(first, b, a)
        flat[2 * i * SHARD : 2 * i * SHARD + SHARD_PAD] = even
        flat[(2 * i + 1) * SHARD : (2 * i + 1) * SHARD + SHARD_PAD] = odd
    for t in range(N_TP):
        for e in range(2):
            rows = flat[pl.ds(2 * t + e, DH, stride=32)]
            w_out[t, :, e * 128 : (e + 1) * 128] = rows.astype(BF16)


def cotangent_kernel(w, att, pieces, keep, give, grad, cols, flat):
    z = lax.axis_index("tp") % 2
    att_now = att[...]
    total = jnp.zeros((384, DH), F32)
    for i in range(N_TP):
        col = 2 * (i // 2) + (z if i % 2 == 0 else 1 - z)
        cot = pieces[i * 384 : (i + 1) * 384]
        cols[col] = dot(att_now, cot, 0, 0)
        total = total + dot(cot, w[col], 1, 1)
    grad[...] = total.astype(BF16)
    for t in range(N_TP):
        for e in range(2):
            flat[pl.ds(2 * t + e, DH, stride=32)] = cols[t, :, e * 128 : (e + 1) * 128]
    flat[FLAT_ROWS:] = jnp.zeros((flat.shape[0] - FLAT_ROWS, 128), F32)
    first = lax.axis_index("ctx") % 2 == 0
    for i in range(CHIPS):
        a = flat[2 * i * SHARD : 2 * i * SHARD + SHARD_PAD]
        b = flat[(2 * i + 1) * SHARD : (2 * i + 1) * SHARD + SHARD_PAD]
        keep[i] = jnp.where(first, a, b)
        give[i] = jnp.where(first, b, a)


def backward_kernel(
    meta, q, kv, prev, nxt, far1, far2, far3, probs, att, out_grad,
    dq, dkv, inner, outer, dfar1, dfar2, dfar3, acc,
):
    far = (far1, far2, far3)
    even = lax.axis_index("ctx") % 2 == 0
    acc[...] = jnp.zeros(acc.shape, F32)
    dkv[...] = jnp.zeros(dkv.shape, F32)
    scale = DH**-0.5
    to_prev = []
    for j in range(3):
        rows = slice(j * BLK, (j + 1) * BLK)
        grad = out_grad[rows]
        keys = select(meta, j, 0, kv, prev, nxt, far)
        vals = select(meta, j, 1, kv, prev, nxt, far)
        delta = jnp.sum(grad.astype(F32) * att[rows].astype(F32), axis=-1, keepdims=True)
        p = probs[j]
        ds = (p * (dot(grad, vals, 1, 1) - delta)).astype(BF16)
        dq[rows] = dot(ds, keys, 1, 0) * scale
        parts = (dot(ds, q[rows], 0, 0) * scale, dot(p.astype(BF16), grad, 0, 0))
        for which in range(2):
            part = parts[which]
            dkv[which, rows] += part[:BLK]
            if j == 0:
                to_prev.append(part[BLK : 2 * BLK])
            else:
                dkv[which, (j - 1) * BLK : j * BLK] += part[BLK : 2 * BLK]
            if j == 2:
                to_next = part[2 * BLK : 3 * BLK]
                inner[which] = jnp.where(even, to_next, to_prev[which]).astype(BF16)
                outer[which] = jnp.where(even, to_prev[which], to_next).astype(BF16)
            else:
                dkv[which, (j + 1) * BLK : (j + 2) * BLK] += part[2 * BLK : 3 * BLK]
            for k in range(3):
                row = pl.multiple_of(meta[3 * j + k] * BLK, BLK)
                acc[k, which, pl.ds(row, BLK)] += part[(3 + k) * BLK : (4 + k) * BLK]
    for k, out in enumerate((dfar1, dfar2, dfar3)):
        out[...] = acc[k].astype(BF16)


def x_parts_kernel(keep, other, far1, far2, far3, out):
    x = lax.axis_index("ctx") // (2 * NZ)
    for i in range(CHIPS):
        row = (i % NZ) * SHARD_PAD
        out[i // NZ, row : row + SHARD_PAD] = (keep[i] + other[i]).astype(BF16)
    out[x, X_FAR:] = jnp.zeros((X_ROWS - X_FAR, DH), BF16)
    for k, far in enumerate((far1, far2, far3)):
        for which in range(2):
            row = X_FAR + which * 384
            out[(x + k + 1) % NX, row : row + 384] = far[which]


def x_sum_kernel(parts, dkv, inner, outer, z_parts, dk, dv):
    even = lax.axis_index("ctx") % 2 == 0
    for i in range(NZ):
        rows = slice(i * SHARD_PAD, (i + 1) * SHARD_PAD)
        chunk = parts[0, rows].astype(F32)
        for x in range(1, NX):
            chunk = chunk + parts[x, rows].astype(F32)
        z_parts[i] = chunk.astype(BF16)
    for which, out in ((0, dk), (1, dv)):
        rows = slice(X_FAR + which * 384, X_FAR + (which + 1) * 384)
        own = dkv[which]
        for x in range(NX):
            own = own + parts[x, rows].astype(F32)
        out[...] = own
        near, away = inner[which].astype(F32), outer[which].astype(F32)
        out[:BLK] += jnp.where(even, away, near)
        out[2 * BLK :] += jnp.where(even, near, away)


def z_sum_kernel(parts, out):
    total = parts[0].astype(F32)
    for i in range(1, NZ):
        total = total + parts[i].astype(F32)
    out[0] = total[:SHARD]


def on_device(queries, key_rows, values, cotangent, w_flat, block_keys):
    ctx = lax.axis_index("ctx")
    tp = lax.axis_index("tp")
    picked = (block_keys[:, 3:] % 3).reshape(9)
    place = jnp.stack([ctx // (2 * NZ), ctx % 2, tp // 2, tp % 2]).astype(jnp.int32)
    meta = jnp.concatenate([picked, place])

    twin = twin_swap(cotangent)
    pieces = lax.all_gather(
        jnp.concatenate([cotangent, twin], axis=0),
        "tp", axis=0, tiled=True, axis_index_groups=Y_GROUPS,
    )
    w_pad = jnp.concatenate([w_flat[0], twin[: SHARD_PAD - SHARD, :128]], axis=0)
    w_own = lax.all_to_all(
        jnp.broadcast_to(w_pad[None], (CHIPS, SHARD_PAD, 128)),
        "ctx", 0, 0, tiled=True, axis_index_groups=SAME_CORE,
    )
    kv = after(jnp.stack([key_rows, values]), twin[0, 0])
    even = ctx % 2 == 0
    prev, nxt = neighbours(kv[:, :BLK], kv[:, 2 * BLK :], even)
    far = [x_shift(kv, -k) for k in (1, 2, 3)]
    arrived = [piece[0, 0, 0] for piece in (prev, nxt, *far)]
    w_other = core_swap(after(w_own, sum(arrived)))
    flat_alloc = N_CTX * SHARD + 8
    weight = pl.pallas_call(
        weight_kernel,
        out_shape=jax.ShapeDtypeStruct((N_TP, DH, WCOL), BF16),
        in_specs=[SMEM, VMEM, VMEM],
        out_specs=VMEM,
        scratch_shapes=[pltpu.VMEM((flat_alloc, 128), F32)],
        compiler_params=PARAMS,
        name="weight_rows",
    )(meta, w_own, w_other)

    probs, att = pl.pallas_call(
        forward_kernel,
        out_shape=(
            jax.ShapeDtypeStruct((3, BLK, 6 * BLK), F32),
            jax.ShapeDtypeStruct((384, DH), BF16),
        ),
        in_specs=[SMEM, ANY] + [VMEM] * 7,
        out_specs=(VMEM, VMEM),
        compiler_params=PARAMS,
        name="attention_forward",
    )(meta, weight, queries, kv, prev, nxt, *far)

    chunk = jax.ShapeDtypeStruct((CHIPS, SHARD_PAD, 128), F32)
    keep, give, out_grad = pl.pallas_call(
        cotangent_kernel,
        out_shape=(chunk, chunk, jax.ShapeDtypeStruct((384, DH), BF16)),
        in_specs=[VMEM, VMEM, VMEM],
        out_specs=(VMEM, VMEM, VMEM),
        scratch_shapes=[
            pltpu.VMEM((N_TP, DH, WCOL), F32),
            pltpu.VMEM((flat_alloc, 128), F32),
        ],
        compiler_params=PARAMS,
        name="cotangent_products",
    )(weight, att, pieces)
    two = (2, 384, DH)
    dq, dkv, inner, outer, *dfar = pl.pallas_call(
        backward_kernel,
        out_shape=(
            jax.ShapeDtypeStruct((384, DH), F32),
            jax.ShapeDtypeStruct(two, F32),
            jax.ShapeDtypeStruct((2, BLK, DH), BF16),
            jax.ShapeDtypeStruct((2, BLK, DH), BF16),
        )
        + (jax.ShapeDtypeStruct(two, BF16),) * 3,
        in_specs=[SMEM] + [VMEM] * 10,
        out_specs=(VMEM,) * 7,
        scratch_shapes=[pltpu.VMEM((3,) + two, F32)],
        compiler_params=PARAMS,
        name="attention_backward",
    )(meta, queries, kv, prev, nxt, *far, probs, att, out_grad)
    x_parts = pl.pallas_call(
        x_parts_kernel,
        out_shape=jax.ShapeDtypeStruct((NX, X_ROWS, DH), BF16),
        compiler_params=PARAMS,
        name="x_parts",
    )(keep, core_swap(give), *dfar)
    from_x = lax.all_to_all(x_parts, "ctx", 0, 0, tiled=True, axis_index_groups=X_GROUPS)
    grad = jax.ShapeDtypeStruct((384, DH), F32)
    z_parts, dk, dv = pl.pallas_call(
        x_sum_kernel,
        out_shape=(
            jax.ShapeDtypeStruct((NZ, SHARD_PAD, 128), BF16),
            grad,
            grad,
        ),
        compiler_params=PARAMS,
        name="x_sum",
    )(from_x, dkv, core_swap(inner), outer_swap(outer))
    from_z = lax.all_to_all(z_parts, "ctx", 0, 0, tiled=True, axis_index_groups=Z_GROUPS)
    weight_grad = pl.pallas_call(
        z_sum_kernel,
        out_shape=jax.ShapeDtypeStruct((1, SHARD, 128), F32),
        compiler_params=PARAMS,
        name="z_sum",
    )(from_z)
    return dq, dk, dv, weight_grad


def solution(mesh):
    in_specs = (
        P("ctx", "tp"),
        P("ctx", "tp"),
        P("ctx", "tp"),
        P("ctx", "tp"),
        P("tp", "ctx", None),
        P("ctx", None),
    )
    out_specs = (P("ctx", "tp"), P("ctx", "tp"), P("ctx", "tp"), P("tp", "ctx", None))
    return jax.shard_map(
        on_device, mesh=mesh, in_specs=in_specs, out_specs=out_specs, check_vma=False
    )
```

```python
import jax
import jax.numpy as jnp
from jax import lax
from jax.experimental import pallas as pl
from jax.experimental.pallas import tpu as pltpu
from jax.sharding import PartitionSpec as P

DH = 128
BLK = 128
F32 = jnp.float32
BF16 = jnp.bfloat16

NX, NZ, NY = 4, 6, 8
N_CTX = NX * NZ * 2
N_TP = NY * 2
CHIPS = NX * NZ
SHARD = 86
SHARD_PAD = 88
FLAT_ROWS = 4096
WCOL = 256
SAME_CORE = [[2 * i + core for i in range(CHIPS)] for core in range(2)]
X_GROUPS = [[x * NZ * 2 + rest for x in range(NX)] for rest in range(NZ * 2)]
Y_GROUPS = [[2 * y + z for y in range(NY)] for z in range(2)]
SMEM = pl.BlockSpec(memory_space=pltpu.SMEM)
VMEM = pl.BlockSpec(memory_space=pltpu.VMEM)
ANY = pl.BlockSpec(memory_space=pl.ANY)
PARAMS = pltpu.CompilerParams(vmem_limit_bytes=12 * 1024 * 1024)

M_X, M_CORE, M_Y, M_Z = 9, 10, 11, 12


def dot(a, b, ca, cb):
    return lax.dot_general(a, b, (((ca,), (cb,)), ((), ())), preferred_element_type=F32)


def x_shift(value, steps):
    pairs = [(s, (s + steps * NZ * 2) % N_CTX) for s in range(N_CTX)]
    return lax.ppermute(value, "ctx", pairs)


def outer_swap(value):
    pairs = [(s, (s - 1 if s % 2 == 0 else s + 1) % N_CTX) for s in range(N_CTX)]
    return lax.ppermute(value, "ctx", pairs)


def neighbours(first, last, even):
    inner = core_swap(jnp.where(even, last, first))
    outer = outer_swap(jnp.where(even, first, last))
    return jnp.where(even, outer, inner), jnp.where(even, inner, outer)


def core_swap(value):
    return lax.ppermute(value, "ctx", [(s, s ^ 1) for s in range(N_CTX)])


def twin_swap(value):
    return lax.ppermute(value, "tp", [(s, s ^ 1) for s in range(N_TP)])


def after(value, element):
    return jnp.where(element < jnp.inf, value, jnp.zeros_like(value))


def select(meta, j, which, kv, prev, nxt, far):
    parts = [kv[which, j * BLK : (j + 1) * BLK]]
    parts.append(prev[which] if j == 0 else kv[which, (j - 1) * BLK : j * BLK])
    parts.append(nxt[which] if j == 2 else kv[which, (j + 1) * BLK : (j + 2) * BLK])
    for k in range(3):
        row = pl.multiple_of(meta[3 * j + k] * BLK, BLK)
        parts.append(far[k][which, pl.ds(row, BLK)])
    return jnp.concatenate(parts, axis=0)


def forward_kernel(meta, w, q, kv, prev, nxt, far1, far2, far3, probs_out, att_out):
    del w
    far = (far1, far2, far3)
    for j in range(3):
        rows = slice(j * BLK, (j + 1) * BLK)
        keys = select(meta, j, 0, kv, prev, nxt, far)
        vals = select(meta, j, 1, kv, prev, nxt, far)
        scores = dot(q[rows], keys, 1, 1) * (DH**-0.5)
        terms = jnp.exp(scores - jnp.max(scores, axis=-1, keepdims=True))
        probs = terms / jnp.sum(terms, axis=-1, keepdims=True)
        probs_out[j] = probs
        att_out[rows] = dot(probs.astype(BF16), vals, 1, 0).astype(BF16)


def weight_kernel(meta, own, other, w_out, flat):
    first = meta[M_CORE] == 0
    for i in range(CHIPS):
        a = own[i].astype(F32)
        b = other[i].astype(F32)
        even = jnp.where(first, a, b)
        odd = jnp.where(first, b, a)
        flat[2 * i * SHARD : 2 * i * SHARD + SHARD_PAD] = even
        flat[(2 * i + 1) * SHARD : (2 * i + 1) * SHARD + SHARD_PAD] = odd
    for t in range(N_TP):
        for e in range(2):
            rows = flat[pl.ds(2 * t + e, DH, stride=32)]
            w_out[t, :, e * 128 : (e + 1) * 128] = rows.astype(BF16)


def cotangent_kernel(w, att, pieces, keep, give, grad, cols, flat):
    z = lax.axis_index("tp") % 2
    att_now = att[...]
    total = jnp.zeros((384, DH), F32)
    for i in range(N_TP):
        col = 2 * (i // 2) + (z if i % 2 == 0 else 1 - z)
        cot = pieces[i * 384 : (i + 1) * 384]
        cols[col] = dot(att_now, cot, 0, 0)
        total = total + dot(cot, w[col], 1, 1)
    grad[...] = total.astype(BF16)
    for t in range(N_TP):
        for e in range(2):
            flat[pl.ds(2 * t + e, DH, stride=32)] = cols[t, :, e * 128 : (e + 1) * 128]
    flat[FLAT_ROWS:] = jnp.zeros((flat.shape[0] - FLAT_ROWS, 128), F32)
    first = lax.axis_index("ctx") % 2 == 0
    for i in range(CHIPS):
        a = flat[2 * i * SHARD : 2 * i * SHARD + SHARD_PAD]
        b = flat[(2 * i + 1) * SHARD : (2 * i + 1) * SHARD + SHARD_PAD]
        keep[i] = jnp.where(first, a, b)
        give[i] = jnp.where(first, b, a)


def backward_kernel(
    meta, q, kv, prev, nxt, far1, far2, far3, probs, att, out_grad,
    dq, dkv, inner, outer, dfar, acc,
):
    far = (far1, far2, far3)
    even = lax.axis_index("ctx") % 2 == 0
    acc[...] = jnp.zeros(acc.shape, F32)
    dkv[...] = jnp.zeros(dkv.shape, F32)
    scale = DH**-0.5
    to_prev = []
    for j in range(3):
        rows = slice(j * BLK, (j + 1) * BLK)
        grad = out_grad[rows]
        keys = select(meta, j, 0, kv, prev, nxt, far)
        vals = select(meta, j, 1, kv, prev, nxt, far)
        delta = jnp.sum(grad.astype(F32) * att[rows].astype(F32), axis=-1, keepdims=True)
        p = probs[j]
        ds = (p * (dot(grad, vals, 1, 1) - delta)).astype(BF16)
        dq[rows] = dot(ds, keys, 1, 0) * scale
        parts = (dot(ds, q[rows], 0, 0) * scale, dot(p.astype(BF16), grad, 0, 0))
        for which in range(2):
            part = parts[which]
            dkv[which, rows] += part[:BLK]
            if j == 0:
                to_prev.append(part[BLK : 2 * BLK])
            else:
                dkv[which, (j - 1) * BLK : j * BLK] += part[BLK : 2 * BLK]
            if j == 2:
                to_next = part[2 * BLK : 3 * BLK]
                inner[which] = jnp.where(even, to_next, to_prev[which]).astype(BF16)
                outer[which] = jnp.where(even, to_prev[which], to_next).astype(BF16)
            else:
                dkv[which, (j + 1) * BLK : (j + 2) * BLK] += part[2 * BLK : 3 * BLK]
            for k in range(3):
                row = pl.multiple_of(meta[3 * j + k] * BLK, BLK)
                acc[k, which, pl.ds(row, BLK)] += part[(3 + k) * BLK : (4 + k) * BLK]
    dfar[...] = acc[...].astype(BF16)


def pair_sum_kernel(keep, other, dkv, out):
    del dkv
    out[...] = (keep[...] + other[...]).astype(BF16)


def chunk_sum_kernel(parts, out):
    total = parts[0].astype(F32)
    for i in range(1, CHIPS):
        total = total + parts[i].astype(F32)
    out[0] = total[:SHARD]


def outer_sum_kernel(dkv, outer, out):
    even = lax.axis_index("ctx") % 2 == 0
    away = outer[...].astype(F32)
    out[...] = dkv[...]
    out[:, :BLK] += jnp.where(even, away, 0.0)
    out[:, 2 * BLK :] += jnp.where(even, 0.0, away)


def last_sum_kernel(total, far1, far2, far3, inner, dk, dv):
    even = lax.axis_index("ctx") % 2 == 0
    for which, out in ((0, dk), (1, dv)):
        parts = [far[which].astype(F32) for far in (far1, far2, far3)]
        out[...] = total[which] + parts[0] + parts[1] + parts[2]
        near = inner[which].astype(F32)
        out[:BLK] += jnp.where(even, 0.0, near)
        out[2 * BLK :] += jnp.where(even, near, 0.0)


def on_device(queries, key_rows, values, cotangent, w_flat, block_keys):
    ctx = lax.axis_index("ctx")
    tp = lax.axis_index("tp")
    picked = (block_keys[:, 3:] % 3).reshape(9)
    place = jnp.stack([ctx // (2 * NZ), ctx % 2, tp // 2, tp % 2]).astype(jnp.int32)
    meta = jnp.concatenate([picked, place])

    twin = twin_swap(cotangent)
    pieces = lax.all_gather(
        jnp.concatenate([cotangent, twin], axis=0),
        "tp", axis=0, tiled=True, axis_index_groups=Y_GROUPS,
    )
    w_pad = jnp.concatenate([w_flat[0], twin[: SHARD_PAD - SHARD, :128]], axis=0)
    w_own = lax.all_to_all(
        jnp.broadcast_to(w_pad[None], (CHIPS, SHARD_PAD, 128)),
        "ctx", 0, 0, tiled=True, axis_index_groups=SAME_CORE,
    )
    kv = after(jnp.stack([key_rows, values]), twin[0, 0])
    even = ctx % 2 == 0
    prev, nxt = neighbours(kv[:, :BLK], kv[:, 2 * BLK :], even)
    far = [x_shift(kv, -k) for k in (1, 2, 3)]
    arrived = [piece[0, 0, 0] for piece in (prev, nxt, *far)]
    w_other = core_swap(after(w_own, sum(arrived)))
    flat_alloc = N_CTX * SHARD + 8
    weight = pl.pallas_call(
        weight_kernel,
        out_shape=jax.ShapeDtypeStruct((N_TP, DH, WCOL), BF16),
        in_specs=[SMEM, VMEM, VMEM],
        out_specs=VMEM,
        scratch_shapes=[pltpu.VMEM((flat_alloc, 128), F32)],
        compiler_params=PARAMS,
        name="weight_rows",
    )(meta, w_own, w_other)

    probs, att = pl.pallas_call(
        forward_kernel,
        out_shape=(
            jax.ShapeDtypeStruct((3, BLK, 6 * BLK), F32),
            jax.ShapeDtypeStruct((384, DH), BF16),
        ),
        in_specs=[SMEM, ANY] + [VMEM] * 7,
        out_specs=(VMEM, VMEM),
        compiler_params=PARAMS,
        name="attention_forward",
    )(meta, weight, queries, kv, prev, nxt, *far)

    chunk = jax.ShapeDtypeStruct((CHIPS, SHARD_PAD, 128), F32)
    keep, give, out_grad = pl.pallas_call(
        cotangent_kernel,
        out_shape=(chunk, chunk, jax.ShapeDtypeStruct((384, DH), BF16)),
        in_specs=[VMEM, VMEM, VMEM],
        out_specs=(VMEM, VMEM, VMEM),
        scratch_shapes=[
            pltpu.VMEM((N_TP, DH, WCOL), F32),
            pltpu.VMEM((flat_alloc, 128), F32),
        ],
        compiler_params=PARAMS,
        name="cotangent_products",
    )(weight, att, pieces)
    two = (2, 384, DH)
    dq, dkv, inner, outer, dfar = pl.pallas_call(
        backward_kernel,
        out_shape=(
            jax.ShapeDtypeStruct((384, DH), F32),
            jax.ShapeDtypeStruct(two, F32),
            jax.ShapeDtypeStruct((2, BLK, DH), BF16),
            jax.ShapeDtypeStruct((2, BLK, DH), BF16),
            jax.ShapeDtypeStruct((3,) + two, BF16),
        ),
        in_specs=[SMEM] + [VMEM] * 10,
        out_specs=(VMEM,) * 5,
        scratch_shapes=[pltpu.VMEM((3,) + two, F32)],
        compiler_params=PARAMS,
        name="attention_backward",
    )(meta, queries, kv, prev, nxt, *far, probs, att, out_grad)
    pair_sum = pl.pallas_call(
        pair_sum_kernel,
        out_shape=jax.ShapeDtypeStruct((CHIPS, SHARD_PAD, 128), BF16),
        in_specs=[VMEM, VMEM, ANY],
        out_specs=VMEM,
        compiler_params=PARAMS,
        name="pair_sum",
    )(keep, core_swap(give), dkv)
    spread = lax.all_to_all(
        pair_sum, "ctx", 0, 0, tiled=True, axis_index_groups=SAME_CORE
    )
    weight_grad = pl.pallas_call(
        chunk_sum_kernel,
        out_shape=jax.ShapeDtypeStruct((1, SHARD, 128), F32),
        compiler_params=PARAMS,
        name="chunk_sum",
    )(spread)
    total = pl.pallas_call(
        outer_sum_kernel,
        out_shape=jax.ShapeDtypeStruct(two, F32),
        compiler_params=PARAMS,
        name="outer_sum",
    )(dkv, outer_swap(outer))
    grad = jax.ShapeDtypeStruct((384, DH), F32)
    dk, dv = pl.pallas_call(
        last_sum_kernel,
        out_shape=(grad, grad),
        compiler_params=PARAMS,
        name="last_sum",
    )(total, *[x_shift(dfar[k], k + 1) for k in range(3)], core_swap(inner))
    return dq, dk, dv, weight_grad


def solution(mesh):
    in_specs = (
        P("ctx", "tp"),
        P("ctx", "tp"),
        P("ctx", "tp"),
        P("ctx", "tp"),
        P("tp", "ctx", None),
        P("ctx", None),
    )
    out_specs = (P("ctx", "tp"), P("ctx", "tp"), P("ctx", "tp"), P("tp", "ctx", None))
    return jax.shard_map(
        on_device, mesh=mesh, in_specs=in_specs, out_specs=out_specs, check_vma=False
    )
```

```python
import jax
import jax.numpy as jnp
from jax import lax
from jax.experimental import pallas as pl
from jax.experimental.pallas import tpu as pltpu
from jax.sharding import PartitionSpec as P

DH = 128
BLK = 128
F32 = jnp.float32
BF16 = jnp.bfloat16

NX, NZ, NY = 4, 6, 8
N_CTX = NX * NZ * 2
N_TP = NY * 2
CHIPS = NX * NZ
SHARD = 86
SHARD_PAD = 88
FLAT_ROWS = 4096
WCOL = 256
SAME_CORE = [[2 * i + core for i in range(CHIPS)] for core in range(2)]
X_GROUPS = [[x * NZ * 2 + rest for x in range(NX)] for rest in range(NZ * 2)]
Y_GROUPS = [[2 * y + z for y in range(NY)] for z in range(2)]
SMEM = pl.BlockSpec(memory_space=pltpu.SMEM)
VMEM = pl.BlockSpec(memory_space=pltpu.VMEM)
ANY = pl.BlockSpec(memory_space=pl.ANY)
PARAMS = pltpu.CompilerParams(vmem_limit_bytes=12 * 1024 * 1024)

M_X, M_CORE, M_Y, M_Z = 9, 10, 11, 12


def dot(a, b, ca, cb):
    return lax.dot_general(a, b, (((ca,), (cb,)), ((), ())), preferred_element_type=F32)


def x_shift(value, steps):
    pairs = [(s, (s + steps * NZ * 2) % N_CTX) for s in range(N_CTX)]
    return lax.ppermute(value, "ctx", pairs)


def outer_swap(value):
    pairs = [(s, (s - 1 if s % 2 == 0 else s + 1) % N_CTX) for s in range(N_CTX)]
    return lax.ppermute(value, "ctx", pairs)


def neighbours(first, last, even):
    inner = core_swap(jnp.where(even, last, first))
    outer = outer_swap(jnp.where(even, first, last))
    return jnp.where(even, outer, inner), jnp.where(even, inner, outer)


def core_swap(value):
    return lax.ppermute(value, "ctx", [(s, s ^ 1) for s in range(N_CTX)])


def twin_swap(value):
    return lax.ppermute(value, "tp", [(s, s ^ 1) for s in range(N_TP)])


def after(value, element):
    return jnp.where(element < jnp.inf, value, jnp.zeros_like(value))


def select(meta, j, which, kv, prev, nxt, far):
    parts = [kv[which, j * BLK : (j + 1) * BLK]]
    parts.append(prev[which] if j == 0 else kv[which, (j - 1) * BLK : j * BLK])
    parts.append(nxt[which] if j == 2 else kv[which, (j + 1) * BLK : (j + 2) * BLK])
    for k in range(3):
        row = pl.multiple_of(meta[3 * j + k] * BLK, BLK)
        parts.append(far[k][which, pl.ds(row, BLK)])
    return jnp.concatenate(parts, axis=0)


def forward_kernel(meta, w, q, kv, prev, nxt, far1, far2, far3, probs_out, att_out):
    del w
    far = (far1, far2, far3)
    for j in range(3):
        rows = slice(j * BLK, (j + 1) * BLK)
        keys = select(meta, j, 0, kv, prev, nxt, far)
        vals = select(meta, j, 1, kv, prev, nxt, far)
        scores = dot(q[rows], keys, 1, 1) * (DH**-0.5)
        terms = jnp.exp(scores - jnp.max(scores, axis=-1, keepdims=True))
        probs = terms / jnp.sum(terms, axis=-1, keepdims=True)
        probs_out[j] = probs
        att_out[rows] = dot(probs.astype(BF16), vals, 1, 0).astype(BF16)


def weight_kernel(meta, own, other, w_out, flat):
    first = meta[M_CORE] == 0
    for i in range(CHIPS):
        a = own[i].astype(F32)
        b = other[i].astype(F32)
        even = jnp.where(first, a, b)
        odd = jnp.where(first, b, a)
        flat[2 * i * SHARD : 2 * i * SHARD + SHARD_PAD] = even
        flat[(2 * i + 1) * SHARD : (2 * i + 1) * SHARD + SHARD_PAD] = odd
    for t in range(N_TP):
        for e in range(2):
            rows = flat[pl.ds(2 * t + e, DH, stride=32)]
            w_out[t, :, e * 128 : (e + 1) * 128] = rows.astype(BF16)


def cotangent_kernel(w, att, pieces, keep, give, grad, att_out, cols, flat):
    z = lax.axis_index("tp") % 2
    att_now = att[...]
    att_out[...] = att_now
    total = jnp.zeros((384, DH), F32)
    for i in range(N_TP):
        col = 2 * (i // 2) + (z if i % 2 == 0 else 1 - z)
        cot = pieces[i * 384 : (i + 1) * 384]
        cols[col] = dot(att_now, cot, 0, 0)
        total = total + dot(cot, w[col], 1, 1)
    grad[...] = total.astype(BF16)
    for t in range(N_TP):
        for e in range(2):
            flat[pl.ds(2 * t + e, DH, stride=32)] = cols[t, :, e * 128 : (e + 1) * 128]
    flat[FLAT_ROWS:] = jnp.zeros((flat.shape[0] - FLAT_ROWS, 128), F32)
    first = lax.axis_index("ctx") % 2 == 0
    for i in range(CHIPS):
        a = flat[2 * i * SHARD : 2 * i * SHARD + SHARD_PAD]
        b = flat[(2 * i + 1) * SHARD : (2 * i + 1) * SHARD + SHARD_PAD]
        keep[i] = jnp.where(first, a, b)
        give[i] = jnp.where(first, b, a)


def backward_kernel(
    meta, q, kv, prev, nxt, far1, far2, far3, probs, att, out_grad,
    dq, dkv, band, dfar, acc,
):
    far = (far1, far2, far3)
    even = lax.axis_index("ctx") % 2 == 0
    acc[...] = jnp.zeros(acc.shape, F32)
    dkv[...] = jnp.zeros(dkv.shape, F32)
    scale = DH**-0.5
    to_prev = []
    for j in range(3):
        rows = slice(j * BLK, (j + 1) * BLK)
        grad = out_grad[rows]
        keys = select(meta, j, 0, kv, prev, nxt, far)
        vals = select(meta, j, 1, kv, prev, nxt, far)
        delta = jnp.sum(grad.astype(F32) * att[rows].astype(F32), axis=-1, keepdims=True)
        p = probs[j]
        ds = (p * (dot(grad, vals, 1, 1) - delta)).astype(BF16)
        dq[rows] = dot(ds, keys, 1, 0) * scale
        parts = (dot(ds, q[rows], 0, 0) * scale, dot(p.astype(BF16), grad, 0, 0))
        for which in range(2):
            part = parts[which]
            dkv[which, rows] += part[:BLK]
            if j == 0:
                to_prev.append(part[BLK : 2 * BLK])
            else:
                dkv[which, (j - 1) * BLK : j * BLK] += part[BLK : 2 * BLK]
            if j == 2:
                to_next = part[2 * BLK : 3 * BLK]
                inner = jnp.where(even, to_next, to_prev[which])
                outer = jnp.where(even, to_prev[which], to_next)
                band[which, :BLK] = outer.astype(BF16)
                band[which, BLK:] = inner.astype(BF16)
            else:
                dkv[which, (j + 1) * BLK : (j + 2) * BLK] += part[2 * BLK : 3 * BLK]
            for k in range(3):
                row = pl.multiple_of(meta[3 * j + k] * BLK, BLK)
                acc[k, which, pl.ds(row, BLK)] += part[(3 + k) * BLK : (4 + k) * BLK]
    dfar[...] = acc[...].astype(BF16)


def pair_sum_kernel(keep, other, dkv, out):
    del dkv
    out[...] = (keep[...] + other[...]).astype(BF16)


def chunk_sum_kernel(parts, out):
    total = parts[0].astype(F32)
    for i in range(1, CHIPS):
        total = total + parts[i].astype(F32)
    out[0] = total[:SHARD]


def grad_sum_kernel(dkv, prev, nxt, far1, far2, far3, inner, dk, dv):
    even = lax.axis_index("ctx") % 2 == 0
    for which, out in ((0, dk), (1, dv)):
        parts = [far[which].astype(F32) for far in (far1, far2, far3)]
        out[...] = dkv[which] + parts[0] + parts[1] + parts[2]
        near = inner[which].astype(F32)
        out[:BLK] += prev[which].astype(F32) + jnp.where(even, 0.0, near)
        out[2 * BLK :] += nxt[which].astype(F32) + jnp.where(even, near, 0.0)


def on_device(queries, key_rows, values, cotangent, w_flat, block_keys):
    ctx = lax.axis_index("ctx")
    tp = lax.axis_index("tp")
    picked = (block_keys[:, 3:] % 3).reshape(9)
    place = jnp.stack([ctx // (2 * NZ), ctx % 2, tp // 2, tp % 2]).astype(jnp.int32)
    meta = jnp.concatenate([picked, place])

    twin = twin_swap(cotangent)
    pieces = lax.all_gather(
        jnp.concatenate([cotangent, twin], axis=0),
        "tp", axis=0, tiled=True, axis_index_groups=Y_GROUPS,
    )
    w_pad = jnp.concatenate([w_flat[0], twin[: SHARD_PAD - SHARD, :128]], axis=0)
    w_own = lax.all_to_all(
        jnp.broadcast_to(w_pad[None], (CHIPS, SHARD_PAD, 128)),
        "ctx", 0, 0, tiled=True, axis_index_groups=SAME_CORE,
    )
    kv = after(jnp.stack([key_rows, values]), twin[0, 0])
    even = ctx % 2 == 0
    prev, nxt = neighbours(kv[:, :BLK], kv[:, 2 * BLK :], even)
    far = [x_shift(kv, -k) for k in (1, 2, 3)]
    arrived = [piece[0, 0, 0] for piece in (prev, nxt, *far)]
    w_other = core_swap(after(w_own, sum(arrived)))
    flat_alloc = N_CTX * SHARD + 8
    weight = pl.pallas_call(
        weight_kernel,
        out_shape=jax.ShapeDtypeStruct((N_TP, DH, WCOL), BF16),
        in_specs=[SMEM, VMEM, VMEM],
        out_specs=VMEM,
        scratch_shapes=[pltpu.VMEM((flat_alloc, 128), F32)],
        compiler_params=PARAMS,
        name="weight_rows",
    )(meta, w_own, w_other)

    probs, att = pl.pallas_call(
        forward_kernel,
        out_shape=(
            jax.ShapeDtypeStruct((3, BLK, 6 * BLK), F32),
            jax.ShapeDtypeStruct((384, DH), BF16),
        ),
        in_specs=[SMEM, ANY] + [VMEM] * 7,
        out_specs=(VMEM, VMEM),
        compiler_params=PARAMS,
        name="attention_forward",
    )(meta, weight, queries, kv, prev, nxt, *far)

    chunk = jax.ShapeDtypeStruct((CHIPS, SHARD_PAD, 128), F32)
    keep, give, out_grad, att_here = pl.pallas_call(
        cotangent_kernel,
        out_shape=(chunk, chunk) + (jax.ShapeDtypeStruct((384, DH), BF16),) * 2,
        in_specs=[VMEM, VMEM, VMEM],
        out_specs=(VMEM,) * 4,
        scratch_shapes=[
            pltpu.VMEM((N_TP, DH, WCOL), F32),
            pltpu.VMEM((flat_alloc, 128), F32),
        ],
        compiler_params=PARAMS,
        name="cotangent_products",
    )(weight, att, pieces)
    two = (2, 384, DH)
    dq, dkv, band, dfar = pl.pallas_call(
        backward_kernel,
        out_shape=(
            jax.ShapeDtypeStruct((384, DH), F32),
            jax.ShapeDtypeStruct(two, F32),
            jax.ShapeDtypeStruct((2, 2 * BLK, DH), BF16),
            jax.ShapeDtypeStruct((3,) + two, BF16),
        ),
        in_specs=[SMEM] + [VMEM] * 10,
        out_specs=(VMEM,) * 4,
        scratch_shapes=[pltpu.VMEM((3,) + two, F32)],
        compiler_params=PARAMS,
        name="attention_backward",
    )(meta, queries, kv, prev, nxt, *far, probs, att_here, out_grad)
    pair_sum = pl.pallas_call(
        pair_sum_kernel,
        out_shape=jax.ShapeDtypeStruct((CHIPS, SHARD_PAD, 128), BF16),
        in_specs=[VMEM, VMEM, ANY],
        out_specs=VMEM,
        compiler_params=PARAMS,
        name="pair_sum",
    )(keep, core_swap(give), dkv)
    spread = lax.all_to_all(
        pair_sum, "ctx", 0, 0, tiled=True, axis_index_groups=SAME_CORE
    )
    weight_grad = pl.pallas_call(
        chunk_sum_kernel,
        out_shape=jax.ShapeDtypeStruct((1, SHARD, 128), F32),
        compiler_params=PARAMS,
        name="chunk_sum",
    )(spread)
    far_back = [x_shift(dfar[k], k + 1) for k in range(3)]
    from_inner = core_swap(band[:, BLK:])
    from_outer = outer_swap(band[:, :BLK])
    zeros = jnp.zeros_like(from_outer)
    from_prev = jnp.where(even, from_outer, zeros)
    from_next = jnp.where(even, zeros, from_outer)
    grad = jax.ShapeDtypeStruct((384, DH), F32)
    dk, dv = pl.pallas_call(
        grad_sum_kernel,
        out_shape=(grad, grad),
        compiler_params=PARAMS,
        name="grad_sum",
    )(dkv, from_prev, from_next, far_back[1], far_back[0], far_back[2], from_inner)
    return dq, dk, dv, weight_grad


def solution(mesh):
    in_specs = (
        P("ctx", "tp"),
        P("ctx", "tp"),
        P("ctx", "tp"),
        P("ctx", "tp"),
        P("tp", "ctx", None),
        P("ctx", None),
    )
    out_specs = (P("ctx", "tp"), P("ctx", "tp"), P("ctx", "tp"), P("tp", "ctx", None))
    return jax.shard_map(
        on_device, mesh=mesh, in_specs=in_specs, out_specs=out_specs, check_vma=False
    )
```

```python
import jax
import jax.numpy as jnp
from jax import lax
from jax.experimental import pallas as pl
from jax.experimental.pallas import tpu as pltpu
from jax.sharding import PartitionSpec as P

DH = 128
BLK = 128
F32 = jnp.float32
BF16 = jnp.bfloat16

NX, NZ, NY = 4, 6, 8
N_CTX = NX * NZ * 2
N_TP = NY * 2
CHIPS = NX * NZ
SHARD = 86
SHARD_PAD = 88
FLAT_ROWS = 4096
WCOL = 256
SAME_CORE = [[2 * i + core for i in range(CHIPS)] for core in range(2)]
X_GROUPS = [[x * NZ * 2 + rest for x in range(NX)] for rest in range(NZ * 2)]
Y_GROUPS = [[2 * y + z for y in range(NY)] for z in range(2)]
SMEM = pl.BlockSpec(memory_space=pltpu.SMEM)
VMEM = pl.BlockSpec(memory_space=pltpu.VMEM)
ANY = pl.BlockSpec(memory_space=pl.ANY)
PARAMS = pltpu.CompilerParams(vmem_limit_bytes=12 * 1024 * 1024)

M_X, M_CORE, M_Y, M_Z = 9, 10, 11, 12


def dot(a, b, ca, cb):
    return lax.dot_general(a, b, (((ca,), (cb,)), ((), ())), preferred_element_type=F32)


def x_shift(value, steps):
    pairs = [(s, (s + steps * NZ * 2) % N_CTX) for s in range(N_CTX)]
    return lax.ppermute(value, "ctx", pairs)


def outer_swap(value):
    pairs = [(s, (s - 1 if s % 2 == 0 else s + 1) % N_CTX) for s in range(N_CTX)]
    return lax.ppermute(value, "ctx", pairs)


def neighbours(first, last, even):
    inner = core_swap(jnp.where(even, last, first))
    outer = outer_swap(jnp.where(even, first, last))
    return jnp.where(even, outer, inner), jnp.where(even, inner, outer)


def core_swap(value):
    return lax.ppermute(value, "ctx", [(s, s ^ 1) for s in range(N_CTX)])


def twin_swap(value):
    return lax.ppermute(value, "tp", [(s, s ^ 1) for s in range(N_TP)])


def after(value, element):
    return jnp.where(element < jnp.inf, value, jnp.zeros_like(value))


def select(meta, j, which, kv, prev, nxt, far):
    parts = [kv[which, j * BLK : (j + 1) * BLK]]
    parts.append(prev[which] if j == 0 else kv[which, (j - 1) * BLK : j * BLK])
    parts.append(nxt[which] if j == 2 else kv[which, (j + 1) * BLK : (j + 2) * BLK])
    for k in range(3):
        row = pl.multiple_of(meta[3 * j + k] * BLK, BLK)
        parts.append(far[k][which, pl.ds(row, BLK)])
    return jnp.concatenate(parts, axis=0)


def forward_kernel(meta, w, q, kv, prev, nxt, far1, far2, far3, probs_out, att_out):
    del w
    far = (far1, far2, far3)
    for j in range(3):
        rows = slice(j * BLK, (j + 1) * BLK)
        keys = select(meta, j, 0, kv, prev, nxt, far)
        vals = select(meta, j, 1, kv, prev, nxt, far)
        scores = dot(q[rows], keys, 1, 1) * (DH**-0.5)
        terms = jnp.exp(scores - jnp.max(scores, axis=-1, keepdims=True))
        probs = terms / jnp.sum(terms, axis=-1, keepdims=True)
        probs_out[j] = probs
        att_out[rows] = dot(probs.astype(BF16), vals, 1, 0).astype(BF16)


def weight_kernel(meta, own, other, w_out, flat):
    first = meta[M_CORE] == 0
    for i in range(CHIPS):
        a = own[i].astype(F32)
        b = other[i].astype(F32)
        even = jnp.where(first, a, b)
        odd = jnp.where(first, b, a)
        flat[2 * i * SHARD : 2 * i * SHARD + SHARD_PAD] = even
        flat[(2 * i + 1) * SHARD : (2 * i + 1) * SHARD + SHARD_PAD] = odd
    for t in range(N_TP):
        for e in range(2):
            rows = flat[pl.ds(2 * t + e, DH, stride=32)]
            w_out[t, :, e * 128 : (e + 1) * 128] = rows.astype(BF16)


def cotangent_kernel(w, att, pieces, keep, give, grad, att_out, cols, flat):
    z = lax.axis_index("tp") % 2
    att_now = att[...]
    att_out[...] = att_now
    total = jnp.zeros((384, DH), F32)
    for i in range(N_TP):
        col = 2 * (i // 2) + (z if i % 2 == 0 else 1 - z)
        cot = pieces[i * 384 : (i + 1) * 384]
        cols[col] = dot(att_now, cot, 0, 0)
        total = total + dot(cot, w[col], 1, 1)
    grad[...] = total.astype(BF16)
    for t in range(N_TP):
        for e in range(2):
            flat[pl.ds(2 * t + e, DH, stride=32)] = cols[t, :, e * 128 : (e + 1) * 128]
    flat[FLAT_ROWS:] = jnp.zeros((flat.shape[0] - FLAT_ROWS, 128), F32)
    first = lax.axis_index("ctx") % 2 == 0
    for i in range(CHIPS):
        a = flat[2 * i * SHARD : 2 * i * SHARD + SHARD_PAD]
        b = flat[(2 * i + 1) * SHARD : (2 * i + 1) * SHARD + SHARD_PAD]
        keep[i] = jnp.where(first, a, b)
        give[i] = jnp.where(first, b, a)


def backward_kernel(
    meta, q, kv, prev, nxt, far1, far2, far3, probs, att, out_grad,
    dq, band, dkv,
):
    far = (far1, far2, far3)
    even = lax.axis_index("ctx") % 2 == 0
    x = lax.axis_index("ctx") // (2 * NZ)
    dkv[...] = jnp.zeros(dkv.shape, F32)
    scale = DH**-0.5
    to_prev = []
    for j in range(3):
        rows = slice(j * BLK, (j + 1) * BLK)
        grad = out_grad[rows]
        keys = select(meta, j, 0, kv, prev, nxt, far)
        vals = select(meta, j, 1, kv, prev, nxt, far)
        delta = jnp.sum(grad.astype(F32) * att[rows].astype(F32), axis=-1, keepdims=True)
        p = probs[j]
        ds = (p * (dot(grad, vals, 1, 1) - delta)).astype(BF16)
        dq[rows] = dot(ds, keys, 1, 0) * scale
        parts = (dot(ds, q[rows], 0, 0) * scale, dot(p.astype(BF16), grad, 0, 0))
        for which in range(2):
            part = parts[which]
            dkv[x, which, rows] += part[:BLK]
            if j == 0:
                to_prev.append(part[BLK : 2 * BLK])
            else:
                dkv[x, which, (j - 1) * BLK : j * BLK] += part[BLK : 2 * BLK]
            if j == 2:
                to_next = part[2 * BLK : 3 * BLK]
                inner = jnp.where(even, to_next, to_prev[which])
                outer = jnp.where(even, to_prev[which], to_next)
                band[which, :BLK] = outer.astype(BF16)
                band[which, BLK:] = inner.astype(BF16)
            else:
                dkv[x, which, (j + 1) * BLK : (j + 2) * BLK] += part[2 * BLK : 3 * BLK]
            for k in range(3):
                row = pl.multiple_of(meta[3 * j + k] * BLK, BLK)
                dkv[(x + k + 1) % NX, which, pl.ds(row, BLK)] += part[(3 + k) * BLK : (4 + k) * BLK]


def pair_sum_kernel(keep, other, dkv, out):
    del dkv
    out[...] = (keep[...] + other[...]).astype(BF16)


def chunk_sum_kernel(parts, dk, out):
    del dk
    total = parts[0].astype(F32)
    for i in range(1, CHIPS):
        total = total + parts[i].astype(F32)
    out[0] = total[:SHARD]


def grad_sum_kernel(total, prev, nxt, inner, dk, dv):
    even = lax.axis_index("ctx") % 2 == 0
    for which, out in ((0, dk), (1, dv)):
        out[...] = total[which]
        near = inner[which].astype(F32)
        out[:BLK] += prev[which].astype(F32) + jnp.where(even, 0.0, near)
        out[2 * BLK :] += nxt[which].astype(F32) + jnp.where(even, near, 0.0)


def on_device(queries, key_rows, values, cotangent, w_flat, block_keys):
    ctx = lax.axis_index("ctx")
    tp = lax.axis_index("tp")
    picked = (block_keys[:, 3:] % 3).reshape(9)
    place = jnp.stack([ctx // (2 * NZ), ctx % 2, tp // 2, tp % 2]).astype(jnp.int32)
    meta = jnp.concatenate([picked, place])

    twin = twin_swap(cotangent)
    pieces = lax.all_gather(
        jnp.concatenate([cotangent, twin], axis=0),
        "tp", axis=0, tiled=True, axis_index_groups=Y_GROUPS,
    )
    w_pad = jnp.concatenate([w_flat[0], twin[: SHARD_PAD - SHARD, :128]], axis=0)
    w_own = lax.all_to_all(
        jnp.broadcast_to(w_pad[None], (CHIPS, SHARD_PAD, 128)),
        "ctx", 0, 0, tiled=True, axis_index_groups=SAME_CORE,
    )
    kv = after(jnp.stack([key_rows, values]), twin[0, 0])
    even = ctx % 2 == 0
    prev, nxt = neighbours(kv[:, :BLK], kv[:, 2 * BLK :], even)
    far = [x_shift(kv, -k) for k in (1, 2, 3)]
    arrived = [piece[0, 0, 0] for piece in (prev, nxt, *far)]
    w_other = core_swap(after(w_own, sum(arrived)))
    flat_alloc = N_CTX * SHARD + 8
    weight = pl.pallas_call(
        weight_kernel,
        out_shape=jax.ShapeDtypeStruct((N_TP, DH, WCOL), BF16),
        in_specs=[SMEM, VMEM, VMEM],
        out_specs=VMEM,
        scratch_shapes=[pltpu.VMEM((flat_alloc, 128), F32)],
        compiler_params=PARAMS,
        name="weight_rows",
    )(meta, w_own, w_other)

    probs, att = pl.pallas_call(
        forward_kernel,
        out_shape=(
            jax.ShapeDtypeStruct((3, BLK, 6 * BLK), F32),
            jax.ShapeDtypeStruct((384, DH), BF16),
        ),
        in_specs=[SMEM, ANY] + [VMEM] * 7,
        out_specs=(VMEM, VMEM),
        compiler_params=PARAMS,
        name="attention_forward",
    )(meta, weight, queries, kv, prev, nxt, *far)

    chunk = jax.ShapeDtypeStruct((CHIPS, SHARD_PAD, 128), F32)
    keep, give, out_grad, att_here = pl.pallas_call(
        cotangent_kernel,
        out_shape=(chunk, chunk) + (jax.ShapeDtypeStruct((384, DH), BF16),) * 2,
        in_specs=[VMEM, VMEM, VMEM],
        out_specs=(VMEM,) * 4,
        scratch_shapes=[
            pltpu.VMEM((N_TP, DH, WCOL), F32),
            pltpu.VMEM((flat_alloc, 128), F32),
        ],
        compiler_params=PARAMS,
        name="cotangent_products",
    )(weight, att, pieces)
    two = (2, 384, DH)
    dq, band, dkv = pl.pallas_call(
        backward_kernel,
        out_shape=(
            jax.ShapeDtypeStruct((384, DH), F32),
            jax.ShapeDtypeStruct((2, 2 * BLK, DH), BF16),
            jax.ShapeDtypeStruct((NX,) + two, F32),
        ),
        in_specs=[SMEM] + [VMEM] * 10,
        out_specs=(VMEM,) * 3,
        compiler_params=PARAMS,
        name="attention_backward",
    )(meta, queries, kv, prev, nxt, *far, probs, att_here, out_grad)
    pair_sum = pl.pallas_call(
        pair_sum_kernel,
        out_shape=jax.ShapeDtypeStruct((CHIPS, SHARD_PAD, 128), BF16),
        in_specs=[VMEM, VMEM, ANY],
        out_specs=VMEM,
        compiler_params=PARAMS,
        name="pair_sum",
    )(keep, core_swap(give), dkv)
    spread = lax.all_to_all(
        pair_sum, "ctx", 0, 0, tiled=True, axis_index_groups=SAME_CORE
    )
    total = lax.psum_scatter(
        dkv.reshape(NX * 768, DH), "ctx", scatter_dimension=0, tiled=True,
        axis_index_groups=X_GROUPS,
    ).reshape(two)
    from_inner = core_swap(band[:, BLK:])
    from_outer = outer_swap(band[:, :BLK])
    zeros = jnp.zeros_like(from_outer)
    from_prev = jnp.where(even, from_outer, zeros)
    from_next = jnp.where(even, zeros, from_outer)
    grad = jax.ShapeDtypeStruct((384, DH), F32)
    dk, dv = pl.pallas_call(
        grad_sum_kernel,
        out_shape=(grad, grad),
        compiler_params=PARAMS,
        name="grad_sum",
    )(total, from_prev, from_next, from_inner)
    weight_grad = pl.pallas_call(
        chunk_sum_kernel,
        out_shape=jax.ShapeDtypeStruct((1, SHARD, 128), F32),
        in_specs=[VMEM, ANY],
        out_specs=VMEM,
        compiler_params=PARAMS,
        name="chunk_sum",
    )(spread, dk)
    return dq, dk, dv, weight_grad


def solution(mesh):
    in_specs = (
        P("ctx", "tp"),
        P("ctx", "tp"),
        P("ctx", "tp"),
        P("ctx", "tp"),
        P("tp", "ctx", None),
        P("ctx", None),
    )
    out_specs = (P("ctx", "tp"), P("ctx", "tp"), P("ctx", "tp"), P("tp", "ctx", None))
    return jax.shard_map(
        on_device, mesh=mesh, in_specs=in_specs, out_specs=out_specs, check_vma=False
    )
```

```python
import jax
import jax.numpy as jnp
from jax import lax
from jax.experimental import pallas as pl
from jax.experimental.pallas import tpu as pltpu
from jax.sharding import PartitionSpec as P

DH = 128
BLK = 128
F32 = jnp.float32
BF16 = jnp.bfloat16

NX, NZ, NY = 4, 6, 8
N_CTX = NX * NZ * 2
N_TP = NY * 2
CHIPS = NX * NZ
SHARD = 86
SHARD_PAD = 88
FLAT_ROWS = 4096
WCOL = 256
SAME_CORE = [[2 * i + core for i in range(CHIPS)] for core in range(2)]
X_GROUPS = [[x * NZ * 2 + rest for x in range(NX)] for rest in range(NZ * 2)]
Y_GROUPS = [[2 * y + z for y in range(NY)] for z in range(2)]
SMEM = pl.BlockSpec(memory_space=pltpu.SMEM)
VMEM = pl.BlockSpec(memory_space=pltpu.VMEM)
ANY = pl.BlockSpec(memory_space=pl.ANY)
PARAMS = pltpu.CompilerParams(vmem_limit_bytes=12 * 1024 * 1024)

STEPS = 4

M_X, M_CORE, M_Y, M_Z = 9, 10, 11, 12


def whole(*shape):
    return pl.BlockSpec(shape, lambda step: (0,) * len(shape), pipeline_mode=pl.Buffered(1))


def dot(a, b, ca, cb):
    return lax.dot_general(a, b, (((ca,), (cb,)), ((), ())), preferred_element_type=F32)


def x_shift(value, steps):
    pairs = [(s, (s + steps * NZ * 2) % N_CTX) for s in range(N_CTX)]
    return lax.ppermute(value, "ctx", pairs)


def outer_swap(value):
    pairs = [(s, (s - 1 if s % 2 == 0 else s + 1) % N_CTX) for s in range(N_CTX)]
    return lax.ppermute(value, "ctx", pairs)


def neighbours(first, last, even):
    inner = core_swap(jnp.where(even, last, first))
    outer = outer_swap(jnp.where(even, first, last))
    return jnp.where(even, outer, inner), jnp.where(even, inner, outer)


def core_swap(value):
    return lax.ppermute(value, "ctx", [(s, s ^ 1) for s in range(N_CTX)])


def twin_swap(value):
    return lax.ppermute(value, "tp", [(s, s ^ 1) for s in range(N_TP)])


def after(value, element):
    return jnp.where(element < jnp.inf, value, jnp.zeros_like(value))


def select(meta, j, which, kv, prev, nxt, far):
    parts = [kv[which, j * BLK : (j + 1) * BLK]]
    parts.append(prev[which] if j == 0 else kv[which, (j - 1) * BLK : j * BLK])
    parts.append(nxt[which] if j == 2 else kv[which, (j + 1) * BLK : (j + 2) * BLK])
    for k in range(3):
        row = pl.multiple_of(meta[3 * j + k] * BLK, BLK)
        parts.append(far[k][which, pl.ds(row, BLK)])
    return jnp.concatenate(parts, axis=0)


def forward_kernel(meta, w, q, kv, prev, nxt, far1, far2, far3, probs_out, att_out):
    del w
    far = (far1, far2, far3)
    for j in range(3):
        rows = slice(j * BLK, (j + 1) * BLK)
        keys = select(meta, j, 0, kv, prev, nxt, far)
        vals = select(meta, j, 1, kv, prev, nxt, far)
        scores = dot(q[rows], keys, 1, 1) * (DH**-0.5)
        terms = jnp.exp(scores - jnp.max(scores, axis=-1, keepdims=True))
        probs = terms / jnp.sum(terms, axis=-1, keepdims=True)
        probs_out[j] = probs
        att_out[rows] = dot(probs.astype(BF16), vals, 1, 0).astype(BF16)


def weight_kernel(meta, own, other, w_out, flat):
    first = meta[M_CORE] == 0
    for i in range(CHIPS):
        a = own[i].astype(F32)
        b = other[i].astype(F32)
        even = jnp.where(first, a, b)
        odd = jnp.where(first, b, a)
        flat[2 * i * SHARD : 2 * i * SHARD + SHARD_PAD] = even
        flat[(2 * i + 1) * SHARD : (2 * i + 1) * SHARD + SHARD_PAD] = odd
    for t in range(N_TP):
        for e in range(2):
            rows = flat[pl.ds(2 * t + e, DH, stride=32)]
            w_out[t, :, e * 128 : (e + 1) * 128] = rows.astype(BF16)


def cotangent_kernel(w, att, pieces, keep, give, grad, att_out, cols, flat, total):
    step = pl.program_id(0)
    z = lax.axis_index("tp") % 2
    att_now = att[...]

    @pl.when(step == 0)
    def _():
        att_out[...] = att_now
        total[...] = jnp.zeros(total.shape, F32)

    here = jnp.zeros((384, DH), F32)
    for i in range(N_TP // STEPS):
        col = 2 * (step * (NY // STEPS) + i // 2) + (z if i % 2 == 0 else 1 - z)
        cot = pieces[i * 384 : (i + 1) * 384]
        cols[col] = dot(att_now, cot, 0, 0)
        here = here + dot(cot, w[col], 1, 1)
    total[...] += here

    @pl.when(step == STEPS - 1)
    def _():
        grad[...] = total[...].astype(BF16)
        for t in range(N_TP):
            for e in range(2):
                flat[pl.ds(2 * t + e, DH, stride=32)] = cols[t, :, e * 128 : (e + 1) * 128]
        flat[FLAT_ROWS:] = jnp.zeros((flat.shape[0] - FLAT_ROWS, 128), F32)
        first = lax.axis_index("ctx") % 2 == 0
        for i in range(CHIPS):
            a = flat[2 * i * SHARD : 2 * i * SHARD + SHARD_PAD]
            b = flat[(2 * i + 1) * SHARD : (2 * i + 1) * SHARD + SHARD_PAD]
            keep[i] = jnp.where(first, a, b)
            give[i] = jnp.where(first, b, a)


def backward_kernel(
    meta, q, kv, prev, nxt, far1, far2, far3, probs, att, out_grad,
    dq, dkv, band, dfar, acc,
):
    far = (far1, far2, far3)
    even = lax.axis_index("ctx") % 2 == 0
    acc[...] = jnp.zeros(acc.shape, F32)
    dkv[...] = jnp.zeros(dkv.shape, F32)
    scale = DH**-0.5
    to_prev = []
    for j in range(3):
        rows = slice(j * BLK, (j + 1) * BLK)
        grad = out_grad[rows]
        keys = select(meta, j, 0, kv, prev, nxt, far)
        vals = select(meta, j, 1, kv, prev, nxt, far)
        delta = jnp.sum(grad.astype(F32) * att[rows].astype(F32), axis=-1, keepdims=True)
        p = probs[j]
        ds = (p * (dot(grad, vals, 1, 1) - delta)).astype(BF16)
        dq[rows] = dot(ds, keys, 1, 0) * scale
        parts = (dot(ds, q[rows], 0, 0) * scale, dot(p.astype(BF16), grad, 0, 0))
        for which in range(2):
            part = parts[which]
            dkv[which, rows] += part[:BLK]
            if j == 0:
                to_prev.append(part[BLK : 2 * BLK])
            else:
                dkv[which, (j - 1) * BLK : j * BLK] += part[BLK : 2 * BLK]
            if j == 2:
                to_next = part[2 * BLK : 3 * BLK]
                inner = jnp.where(even, to_next, to_prev[which])
                outer = jnp.where(even, to_prev[which], to_next)
                band[which, :BLK] = outer.astype(BF16)
                band[which, BLK:] = inner.astype(BF16)
            else:
                dkv[which, (j + 1) * BLK : (j + 2) * BLK] += part[2 * BLK : 3 * BLK]
            for k in range(3):
                row = pl.multiple_of(meta[3 * j + k] * BLK, BLK)
                acc[k, which, pl.ds(row, BLK)] += part[(3 + k) * BLK : (4 + k) * BLK]
    dfar[...] = acc[...].astype(BF16)


def pair_sum_kernel(keep, other, dkv, out):
    del dkv
    out[...] = (keep[...] + other[...]).astype(BF16)


def chunk_sum_kernel(parts, out):
    total = parts[0].astype(F32)
    for i in range(1, CHIPS):
        total = total + parts[i].astype(F32)
    out[...] = total[:SHARD].reshape(SHARD, 1, 128)


def grad_sum_kernel(dkv, prev, nxt, far1, far2, far3, inner, dk, dv):
    even = lax.axis_index("ctx") % 2 == 0
    for which, out in ((0, dk), (1, dv)):
        parts = [far[which].astype(F32) for far in (far1, far2, far3)]
        out[...] = dkv[which] + parts[0] + parts[1] + parts[2]
        near = inner[which].astype(F32)
        out[:BLK] += prev[which].astype(F32) + jnp.where(even, 0.0, near)
        out[2 * BLK :] += nxt[which].astype(F32) + jnp.where(even, near, 0.0)


def on_device(queries, key_rows, values, cotangent, w_flat, block_keys):
    ctx = lax.axis_index("ctx")
    tp = lax.axis_index("tp")
    picked = (block_keys[:, 3:] % 3).reshape(9)
    place = jnp.stack([ctx // (2 * NZ), ctx % 2, tp // 2, tp % 2]).astype(jnp.int32)
    meta = jnp.concatenate([picked, place])

    twin = twin_swap(cotangent)
    pieces = lax.all_gather(
        jnp.concatenate([cotangent, twin], axis=0),
        "tp", axis=0, tiled=True, axis_index_groups=Y_GROUPS,
    )
    w_pad = jnp.concatenate([w_flat[0], twin[: SHARD_PAD - SHARD, :128]], axis=0)
    w_own = lax.all_to_all(
        jnp.broadcast_to(w_pad[None], (CHIPS, SHARD_PAD, 128)),
        "ctx", 0, 0, tiled=True, axis_index_groups=SAME_CORE,
    )
    kv = after(jnp.stack([key_rows, values]), twin[0, 0])
    even = ctx % 2 == 0
    prev, nxt = neighbours(kv[:, :BLK], kv[:, 2 * BLK :], even)
    far = [x_shift(kv, -k) for k in (1, 2, 3)]
    arrived = [piece[0, 0, 0] for piece in (prev, nxt, *far)]
    w_other = core_swap(after(w_own, sum(arrived)))
    flat_alloc = N_CTX * SHARD + 8
    weight = pl.pallas_call(
        weight_kernel,
        out_shape=jax.ShapeDtypeStruct((N_TP, DH, WCOL), BF16),
        in_specs=[SMEM, VMEM, VMEM],
        out_specs=VMEM,
        scratch_shapes=[pltpu.VMEM((flat_alloc, 128), F32)],
        compiler_params=PARAMS,
        name="weight_rows",
    )(meta, w_own, w_other)

    probs, att = pl.pallas_call(
        forward_kernel,
        out_shape=(
            jax.ShapeDtypeStruct((3, BLK, 6 * BLK), F32),
            jax.ShapeDtypeStruct((384, DH), BF16),
        ),
        in_specs=[SMEM, ANY] + [VMEM] * 7,
        out_specs=(VMEM, VMEM),
        compiler_params=PARAMS,
        name="attention_forward",
    )(meta, weight, queries, kv, prev, nxt, *far)

    chunk = jax.ShapeDtypeStruct((CHIPS, SHARD_PAD, 128), F32)
    keep, give, out_grad, att_here = pl.pallas_call(
        cotangent_kernel,
        out_shape=(chunk, chunk) + (jax.ShapeDtypeStruct((384, DH), BF16),) * 2,
        grid=(STEPS,),
        in_specs=[
            whole(N_TP, DH, WCOL),
            whole(384, DH),
            pl.BlockSpec((N_TP * 384 // STEPS, WCOL), lambda step: (step, 0)),
        ],
        out_specs=(
            whole(*chunk.shape),
            whole(*chunk.shape),
            whole(384, DH),
            whole(384, DH),
        ),
        scratch_shapes=[
            pltpu.VMEM((N_TP, DH, WCOL), F32),
            pltpu.VMEM((flat_alloc, 128), F32),
            pltpu.VMEM((384, DH), F32),
        ],
        compiler_params=pltpu.CompilerParams(vmem_limit_bytes=50 * 1024 * 1024),
        name="cotangent_products",
    )(weight, att, pieces)
    two = (2, 384, DH)
    dq, dkv, band, dfar = pl.pallas_call(
        backward_kernel,
        out_shape=(
            jax.ShapeDtypeStruct((384, DH), F32),
            jax.ShapeDtypeStruct(two, F32),
            jax.ShapeDtypeStruct((2, 2 * BLK, DH), BF16),
            jax.ShapeDtypeStruct((3,) + two, BF16),
        ),
        in_specs=[SMEM] + [VMEM] * 10,
        out_specs=(VMEM,) * 4,
        scratch_shapes=[pltpu.VMEM((3,) + two, F32)],
        compiler_params=PARAMS,
        name="attention_backward",
    )(meta, queries, kv, prev, nxt, *far, probs, att_here, out_grad)
    pair_sum = pl.pallas_call(
        pair_sum_kernel,
        out_shape=jax.ShapeDtypeStruct((CHIPS, SHARD_PAD, 128), BF16),
        in_specs=[VMEM, VMEM, ANY],
        out_specs=VMEM,
        compiler_params=PARAMS,
        name="pair_sum",
    )(keep, core_swap(give), dkv)
    spread = lax.all_to_all(
        pair_sum, "ctx", 0, 0, tiled=True, axis_index_groups=SAME_CORE
    )
    weight_grad = pl.pallas_call(
        chunk_sum_kernel,
        out_shape=jax.ShapeDtypeStruct((SHARD, 1, 128), F32),
        compiler_params=PARAMS,
        name="chunk_sum",
    )(spread).transpose(1, 0, 2)
    far_back = [x_shift(dfar[k], k + 1) for k in range(3)]
    from_inner = core_swap(band[:, BLK:])
    from_outer = outer_swap(band[:, :BLK])
    zeros = jnp.zeros_like(from_outer)
    from_prev = jnp.where(even, from_outer, zeros)
    from_next = jnp.where(even, zeros, from_outer)
    grad = jax.ShapeDtypeStruct((384, DH), F32)
    dk, dv = pl.pallas_call(
        grad_sum_kernel,
        out_shape=(grad, grad),
        compiler_params=PARAMS,
        name="grad_sum",
    )(dkv, from_prev, from_next, far_back[1], far_back[0], far_back[2], from_inner)
    return dq, dk, dv, weight_grad


def solution(mesh):
    in_specs = (
        P("ctx", "tp"),
        P("ctx", "tp"),
        P("ctx", "tp"),
        P("ctx", "tp"),
        P("tp", "ctx", None),
        P("ctx", None),
    )
    out_specs = (P("ctx", "tp"), P("ctx", "tp"), P("ctx", "tp"), P("tp", "ctx", None))
    return jax.shard_map(
        on_device, mesh=mesh, in_specs=in_specs, out_specs=out_specs, check_vma=False
    )
```

```python
import jax
import jax.numpy as jnp
from jax import lax
from jax.experimental import pallas as pl
from jax.experimental.pallas import tpu as pltpu
from jax.sharding import PartitionSpec as P

DH = 128
BLK = 128
F32 = jnp.float32
BF16 = jnp.bfloat16

NX, NZ, NY = 4, 6, 8
N_CTX = NX * NZ * 2
N_TP = NY * 2
CHIPS = NX * NZ
SHARD = 86
SHARD_PAD = 88
FLAT_ROWS = 4096
WCOL = 256
SAME_CORE = [[2 * i + core for i in range(CHIPS)] for core in range(2)]
X_GROUPS = [[x * NZ * 2 + rest for x in range(NX)] for rest in range(NZ * 2)]
Y_GROUPS = [[2 * y + z for y in range(NY)] for z in range(2)]
SMEM = pl.BlockSpec(memory_space=pltpu.SMEM)
VMEM = pl.BlockSpec(memory_space=pltpu.VMEM)
ANY = pl.BlockSpec(memory_space=pl.ANY)
PARAMS = pltpu.CompilerParams(vmem_limit_bytes=12 * 1024 * 1024)

M_X, M_CORE, M_Y, M_Z = 9, 10, 11, 12


def dot(a, b, ca, cb):
    return lax.dot_general(a, b, (((ca,), (cb,)), ((), ())), preferred_element_type=F32)


def x_shift(value, steps):
    pairs = [(s, (s + steps * NZ * 2) % N_CTX) for s in range(N_CTX)]
    return lax.ppermute(value, "ctx", pairs)


def outer_swap(value):
    pairs = [(s, (s - 1 if s % 2 == 0 else s + 1) % N_CTX) for s in range(N_CTX)]
    return lax.ppermute(value, "ctx", pairs)


def neighbours(first, last, even):
    inner = core_swap(jnp.where(even, last, first))
    outer = outer_swap(jnp.where(even, first, last))
    return jnp.where(even, outer, inner), jnp.where(even, inner, outer)


def core_swap(value):
    return lax.ppermute(value, "ctx", [(s, s ^ 1) for s in range(N_CTX)])


def twin_swap(value):
    return lax.ppermute(value, "tp", [(s, s ^ 1) for s in range(N_TP)])


def after(value, element):
    return jnp.where(element < jnp.inf, value, jnp.zeros_like(value))


def select(meta, j, which, kv, prev, nxt, far):
    parts = [kv[which, j * BLK : (j + 1) * BLK]]
    parts.append(prev[which] if j == 0 else kv[which, (j - 1) * BLK : j * BLK])
    parts.append(nxt[which] if j == 2 else kv[which, (j + 1) * BLK : (j + 2) * BLK])
    for k in range(3):
        row = pl.multiple_of(meta[3 * j + k] * BLK, BLK)
        parts.append(far[k][which, pl.ds(row, BLK)])
    return jnp.concatenate(parts, axis=0)


def forward_kernel(meta, w, q, kv, prev, nxt, far1, far2, far3, probs_out, att_out):
    del w
    far = (far1, far2, far3)
    for j in range(3):
        rows = slice(j * BLK, (j + 1) * BLK)
        keys = select(meta, j, 0, kv, prev, nxt, far)
        vals = select(meta, j, 1, kv, prev, nxt, far)
        scores = dot(q[rows], keys, 1, 1) * (DH**-0.5)
        terms = jnp.exp(scores - jnp.max(scores, axis=-1, keepdims=True))
        probs = terms / jnp.sum(terms, axis=-1, keepdims=True)
        probs_out[j] = probs
        att_out[rows] = dot(probs.astype(BF16), vals, 1, 0).astype(BF16)


def weight_kernel(meta, own, other, w_out, flat):
    first = meta[M_CORE] == 0
    for i in range(CHIPS):
        a = own[i].astype(F32)
        b = other[i].astype(F32)
        even = jnp.where(first, a, b)
        odd = jnp.where(first, b, a)
        flat[2 * i * SHARD : 2 * i * SHARD + SHARD_PAD] = even
        flat[(2 * i + 1) * SHARD : (2 * i + 1) * SHARD + SHARD_PAD] = odd
    for t in range(N_TP):
        for e in range(2):
            rows = flat[pl.ds(2 * t + e, DH, stride=32)]
            w_out[t, :, e * 128 : (e + 1) * 128] = rows.astype(BF16)


def cotangent_kernel(w, att, pieces, keep, give, grad, att_out, cols, flat):
    z = lax.axis_index("tp") % 2
    att_now = att[...]
    att_out[...] = att_now
    total = jnp.zeros((384, DH), F32)
    for i in range(N_TP):
        col = 2 * (i // 2) + (z if i % 2 == 0 else 1 - z)
        cot = pieces[i * 384 : (i + 1) * 384]
        cols[col] = dot(att_now, cot, 0, 0)
        total = total + dot(cot, w[col], 1, 1)
    grad[...] = total.astype(BF16)
    for t in range(N_TP):
        for e in range(2):
            flat[pl.ds(2 * t + e, DH, stride=32)] = cols[t, :, e * 128 : (e + 1) * 128]
    flat[FLAT_ROWS:] = jnp.zeros((flat.shape[0] - FLAT_ROWS, 128), F32)
    first = lax.axis_index("ctx") % 2 == 0
    for i in range(CHIPS):
        a = flat[2 * i * SHARD : 2 * i * SHARD + SHARD_PAD]
        b = flat[(2 * i + 1) * SHARD : (2 * i + 1) * SHARD + SHARD_PAD]
        keep[i] = jnp.where(first, a, b)
        give[i] = jnp.where(first, b, a)


def backward_kernel(
    meta, q, kv, prev, nxt, far1, far2, far3, probs, att, out_grad,
    dq, dkv, band, dfar, acc,
):
    far = (far1, far2, far3)
    even = lax.axis_index("ctx") % 2 == 0
    acc[...] = jnp.zeros(acc.shape, F32)
    dkv[...] = jnp.zeros(dkv.shape, F32)
    scale = DH**-0.5
    to_prev = []
    for j in range(3):
        rows = slice(j * BLK, (j + 1) * BLK)
        grad = out_grad[rows]
        keys = select(meta, j, 0, kv, prev, nxt, far)
        vals = select(meta, j, 1, kv, prev, nxt, far)
        delta = jnp.sum(grad.astype(F32) * att[rows].astype(F32), axis=-1, keepdims=True)
        p = probs[j]
        ds = (p * (dot(grad, vals, 1, 1) - delta)).astype(BF16)
        dq[rows] = dot(ds, keys, 1, 0) * scale
        parts = (dot(ds, q[rows], 0, 0) * scale, dot(p.astype(BF16), grad, 0, 0))
        for which in range(2):
            part = parts[which]
            dkv[which, rows] += part[:BLK]
            if j == 0:
                to_prev.append(part[BLK : 2 * BLK])
            else:
                dkv[which, (j - 1) * BLK : j * BLK] += part[BLK : 2 * BLK]
            if j == 2:
                to_next = part[2 * BLK : 3 * BLK]
                inner = jnp.where(even, to_next, to_prev[which])
                outer = jnp.where(even, to_prev[which], to_next)
                band[which, :BLK] = outer.astype(BF16)
                band[which, BLK:] = inner.astype(BF16)
            else:
                dkv[which, (j + 1) * BLK : (j + 2) * BLK] += part[2 * BLK : 3 * BLK]
            for k in range(3):
                row = pl.multiple_of(meta[3 * j + k] * BLK, BLK)
                acc[k, which, pl.ds(row, BLK)] += part[(3 + k) * BLK : (4 + k) * BLK]
    dfar[...] = acc[...].astype(BF16)


def pair_sum_kernel(keep, other, dkv, out):
    del dkv
    out[...] = (keep[...] + other[...]).astype(BF16)


def chunk_sum_kernel(parts, out):
    total = parts[0].astype(F32)
    for i in range(1, CHIPS):
        total = total + parts[i].astype(F32)
    out[...] = total[:SHARD].reshape(SHARD, 1, 128)


def grad_sum_kernel(dkv, prev, nxt, far1, far2, far3, inner, dk, dv):
    even = lax.axis_index("ctx") % 2 == 0
    for which, out in ((0, dk), (1, dv)):
        parts = [far[which].astype(F32) for far in (far1, far2, far3)]
        out[...] = dkv[which] + parts[0] + parts[1] + parts[2]
        near = inner[which].astype(F32)
        out[:BLK] += prev[which].astype(F32) + jnp.where(even, 0.0, near)
        out[2 * BLK :] += nxt[which].astype(F32) + jnp.where(even, near, 0.0)


def on_device(queries, key_rows, values, cotangent, w_flat, block_keys):
    ctx = lax.axis_index("ctx")
    tp = lax.axis_index("tp")
    picked = (block_keys[:, 3:] % 3).reshape(9)
    place = jnp.stack([ctx // (2 * NZ), ctx % 2, tp // 2, tp % 2]).astype(jnp.int32)
    meta = jnp.concatenate([picked, place])

    twin = twin_swap(cotangent)
    pieces = lax.all_gather(
        jnp.concatenate([cotangent, twin], axis=0),
        "tp", axis=0, tiled=True, axis_index_groups=Y_GROUPS,
    )
    w_pad = jnp.concatenate([w_flat[0], twin[: SHARD_PAD - SHARD, :128]], axis=0)
    w_own = lax.all_to_all(
        jnp.broadcast_to(w_pad[None], (CHIPS, SHARD_PAD, 128)),
        "ctx", 0, 0, tiled=True, axis_index_groups=SAME_CORE,
    )
    kv = after(jnp.stack([key_rows, values]), twin[0, 0])
    even = ctx % 2 == 0
    prev, nxt = neighbours(kv[:, :BLK], kv[:, 2 * BLK :], even)
    far = [x_shift(kv, -k) for k in (1, 2, 3)]
    arrived = [piece[0, 0, 0] for piece in (prev, nxt, *far)]
    w_other = core_swap(after(w_own, sum(arrived)))
    flat_alloc = N_CTX * SHARD + 8
    weight = pl.pallas_call(
        weight_kernel,
        out_shape=jax.ShapeDtypeStruct((N_TP, DH, WCOL), BF16),
        in_specs=[SMEM, VMEM, VMEM],
        out_specs=VMEM,
        scratch_shapes=[pltpu.VMEM((flat_alloc, 128), F32)],
        compiler_params=PARAMS,
        name="weight_rows",
    )(meta, w_own, w_other)

    probs, att = pl.pallas_call(
        forward_kernel,
        out_shape=(
            jax.ShapeDtypeStruct((3, BLK, 6 * BLK), F32),
            jax.ShapeDtypeStruct((384, DH), BF16),
        ),
        in_specs=[SMEM, ANY] + [VMEM] * 7,
        out_specs=(VMEM, VMEM),
        compiler_params=PARAMS,
        name="attention_forward",
    )(meta, weight, queries, kv, prev, nxt, *far)

    chunk = jax.ShapeDtypeStruct((CHIPS, SHARD_PAD, 128), F32)
    keep, give, out_grad, att_here = pl.pallas_call(
        cotangent_kernel,
        out_shape=(chunk, chunk) + (jax.ShapeDtypeStruct((384, DH), BF16),) * 2,
        in_specs=[VMEM, VMEM, VMEM],
        out_specs=(VMEM,) * 4,
        scratch_shapes=[
            pltpu.VMEM((N_TP, DH, WCOL), F32),
            pltpu.VMEM((flat_alloc, 128), F32),
        ],
        compiler_params=PARAMS,
        name="cotangent_products",
    )(weight, att, pieces)
    two = (2, 384, DH)
    dq, dkv, band, dfar = pl.pallas_call(
        backward_kernel,
        out_shape=(
            jax.ShapeDtypeStruct((384, DH), F32),
            jax.ShapeDtypeStruct(two, F32),
            jax.ShapeDtypeStruct((2, 2 * BLK, DH), BF16),
            jax.ShapeDtypeStruct((3,) + two, BF16),
        ),
        in_specs=[SMEM] + [VMEM] * 10,
        out_specs=(VMEM,) * 4,
        scratch_shapes=[pltpu.VMEM((3,) + two, F32)],
        compiler_params=PARAMS,
        name="attention_backward",
    )(meta, queries, kv, prev, nxt, *far, probs, att_here, out_grad)
    pair_sum = pl.pallas_call(
        pair_sum_kernel,
        out_shape=jax.ShapeDtypeStruct((CHIPS, SHARD_PAD, 128), BF16),
        in_specs=[VMEM, VMEM, ANY],
        out_specs=VMEM,
        compiler_params=PARAMS,
        name="pair_sum",
    )(keep, core_swap(give), dkv)
    spread = lax.all_to_all(
        pair_sum, "ctx", 0, 0, tiled=True, axis_index_groups=SAME_CORE
    )
    weight_grad = pl.pallas_call(
        chunk_sum_kernel,
        out_shape=jax.ShapeDtypeStruct((SHARD, 1, 128), F32),
        compiler_params=PARAMS,
        name="chunk_sum",
    )(spread).transpose(1, 0, 2)
    far_back = [x_shift(dfar[k], k + 1) for k in range(3)]
    from_inner = core_swap(band[:, BLK:])
    from_outer = outer_swap(band[:, :BLK])
    zeros = jnp.zeros_like(from_outer)
    from_prev = jnp.where(even, from_outer, zeros)
    from_next = jnp.where(even, zeros, from_outer)
    grad = jax.ShapeDtypeStruct((384, DH), F32)
    dk, dv = pl.pallas_call(
        grad_sum_kernel,
        out_shape=(grad, grad),
        compiler_params=PARAMS,
        name="grad_sum",
    )(dkv, from_prev, from_next, far_back[1], far_back[0], far_back[2], from_inner)
    return dq, dk, dv, weight_grad


def solution(mesh):
    in_specs = (
        P("ctx", "tp"),
        P("ctx", "tp"),
        P("ctx", "tp"),
        P("ctx", "tp"),
        P("tp", "ctx", None),
        P("ctx", None),
    )
    out_specs = (P("ctx", "tp"), P("ctx", "tp"), P("ctx", "tp"), P("tp", "ctx", None))
    return jax.shard_map(
        on_device, mesh=mesh, in_specs=in_specs, out_specs=out_specs, check_vma=False
    )
```
